128 devices in a mesh: dp: 8 (over y, x_hi), section: 4 (over x_lo, core), mp: 4 (over z).
Axes of the slice: x: 4 (x_hi: 2, x_lo: 2; x = x_hi * 2 + x_lo), y: 4, z: 4, core: 2. Of those that a mesh axis runs over, the one named last changes fastest.
Arguments:
- hidden_in: bfloat16 [16, 128, 4096], P('dp')
- slot_hidden: bfloat16 [4, 16, 16, 4096], P('section', 'dp'), may hold values from -6 to 6
- norm_gain: float32 [4, 4096], P('section'), may hold values from 0.5 to 1.5
- w_query: bfloat16 [4, 4096, 3072], P('section', None, 'mp')
- w_key: bfloat16 [4, 4096, 1024], P('section', None, 'mp')
- w_value: bfloat16 [4, 4096, 1024], P('section', None, 'mp'), may hold values from -0.09375 to 0.09375
- w_out: bfloat16 [4, 3072, 4096], P('section', 'mp'), may hold values from -0.109375 to 0.109375
- key_a: bfloat16 [4, 4096, 64], P('section'), may hold values from -0.09375 to 0.09375
- key_b: bfloat16 [4, 64, 1024], P('section', None, 'mp'), may hold values from -0.375 to 0.375
- value_a: bfloat16 [4, 4096, 64], P('section'), may hold values from -0.09375 to 0.09375
- value_b: bfloat16 [4, 64, 1024], P('section', None, 'mp'), may hold values from -0.375 to 0.375
- cotangent: bfloat16 [16, 128, 4096], P('dp'), may hold values from -6 to 6
Outputs:
- grad_a: float32 [4, 2, 4096, 64], P('section')
- grad_b: float32 [4, 2, 64, 1024], P('section', None, None, 'mp')
The draws below stay inside these ranges and needn't reach their ends.
All inputs are finite; a program needn't handle non-finite values.
Results may differ from the reference program's by a relative error of at most 0.028.
Values may be sent and summed in bfloat16 or wider, within the bound.
No kernel may reach another device: no remote copies, remote signals or barrier semaphores. Data moves between devices by JAX's collectives and lax.ppermute only.
A program may use at most 128 MiB of HBM per device.

```python
import math
import jax
import jax.numpy as jnp
from jax import lax

D = 4096
QH = 24
KVH = 8
HD = 128
SLOTS = 16
RANK = 64
BLOCK = 128
LAYERS = 4
BLOCKS = 16


def key_query(key):
    streams = jax.random.split(jax.random.fold_in(key, 17), 2)
    key_weights = jax.random.normal(streams[0], (LAYERS, D, KVH * HD), jnp.float32) / math.sqrt(D)
    query_weights = jax.random.normal(streams[1], (LAYERS, D, QH * HD), jnp.float32) / math.sqrt(D)
    return (key_weights, query_weights)


def draw_w_key(key, part):
    return key_query(key)[0].astype(jnp.bfloat16)


def draw_w_query(key, part):
    return key_query(key)[1].astype(jnp.bfloat16)


def draw_hidden_in(key, part):
    streams = jax.random.split(jax.random.fold_in(key, 3), 3)
    values = jax.random.normal(streams[0], (BLOCKS, BLOCK, D), jnp.float32)
    scales = jnp.exp(jax.random.uniform(streams[2], (BLOCKS, BLOCK, 1), jnp.float32, 0.0, math.log(10.0)))
    return (values * scales).astype(jnp.bfloat16)


def level_of(rng, extent, shards, least, largest):
    level = 1.0
    for dim, shards_of in shards:
        heights = jax.random.uniform(jax.random.fold_in(jax.random.fold_in(rng, 6), dim), (shards_of,), jnp.float32, least / len(shards), largest / len(shards))
        level = level * jnp.repeat(jnp.exp(heights), extent[dim] // shards_of).reshape((-1,) + (1,) * (len(extent) - 1 - dim))
    return level


def centred(stream_key, shape, deviation, reach, shards=(), kind=jnp.bfloat16):
    drawn = deviation * jax.random.normal(stream_key, shape, jnp.float32)
    if shards:
        drawn = drawn * level_of(stream_key, shape, shards, -0.22, 0.18)
    return jnp.clip(drawn, -reach, reach).astype(kind)


def setup_inputs(seed: int = 0) -> dict:
    splits = jax.random.split(jax.random.key(seed), 13)
    hidden_in = draw_hidden_in(jax.random.fold_in(splits[12], 71), 0)
    slot_hidden = centred(splits[1], (LAYERS, BLOCKS, SLOTS, D), 1.0, 6.0, ((0, 4), (1, 8)))
    norm_gain = jnp.clip(1.0 + 0.1 * jax.random.normal(splits[2], (LAYERS, D), jnp.float32), 0.5, 1.5)
    w_query = draw_w_query(jax.random.fold_in(splits[12], 71), 0)
    w_key = draw_w_key(jax.random.fold_in(splits[12], 71), 0)
    w_value = centred(splits[5], (LAYERS, D, KVH * HD), D ** -0.5, 0.09375, ((0, 4), (2, 4)))
    w_out = centred(splits[6], (LAYERS, QH * HD, D), (QH * HD) ** -0.5, 0.109375, ((0, 4), (1, 4)))
    key_a = centred(splits[7], (LAYERS, D, RANK), D ** -0.5, 0.09375, ((0, 4),))
    key_b = centred(splits[8], (LAYERS, RANK, KVH * HD), (4 * RANK) ** -0.5, 0.375, ((0, 4), (2, 4)))
    value_a = centred(splits[9], (LAYERS, D, RANK), D ** -0.5, 0.09375, ((0, 4),))
    value_b = centred(splits[10], (LAYERS, RANK, KVH * HD), (4 * RANK) ** -0.5, 0.375, ((0, 4), (2, 4)))
    cotangent = centred(splits[11], (BLOCKS, BLOCK, D), 1.0, 6.0, ((0, 8),))
    return dict(hidden_in=hidden_in, slot_hidden=slot_hidden, norm_gain=norm_gain, w_query=w_query, w_key=w_key, w_value=w_value, w_out=w_out, key_a=key_a, key_b=key_b, value_a=value_a, value_b=value_b, cotangent=cotangent)


EPS = 1e-05
NEG = -1e+30
HIGH = lax.Precision.HIGHEST

def normalize(rows):
    wide = rows.astype(jnp.float32)
    inverse = lax.rsqrt(lax.optimization_barrier(jnp.mean(wide * wide, axis=-1, keepdims=True)) + EPS)
    return (wide * inverse, inverse)

def visible(count, slots):
    qpos = lax.broadcasted_iota(jnp.int32, (count, slots + count), 0)
    kpos = lax.broadcasted_iota(jnp.int32, (count, slots + count), 1)
    return (kpos < slots) | (kpos - slots <= qpos)

def mixdot(left, right):
    return jnp.dot(left, right, preferred_element_type=jnp.float32)

def attend(query, keys, values):
    query, keys, values = lax.optimization_barrier((query, keys, values))
    count = query.shape[0]
    groups = keys.shape[1] // HD
    per_group = query.shape[1] // keys.shape[1]
    q_four = query.astype(jnp.float32).reshape(count, groups, per_group, HD)
    k_three = keys.astype(jnp.float32).reshape(-1, groups, HD)
    v_three = values.astype(jnp.float32).reshape(-1, groups, HD)
    scores = jnp.einsum('igcd,jgd->gcij', q_four, k_three, precision=HIGH) / math.sqrt(HD)
    scores = jnp.where(visible(count, SLOTS), scores, NEG)
    top = lax.optimization_barrier(jnp.max(scores, axis=-1, keepdims=True))
    probs = jnp.exp(scores - top)
    probs = probs / lax.optimization_barrier(jnp.sum(probs, axis=-1, keepdims=True))
    weights = lax.optimization_barrier(probs.astype(jnp.bfloat16))
    mixed = jnp.einsum('gcij,jgd->igcd', weights.astype(jnp.float32), v_three, precision=HIGH)
    return (mixed.reshape(count, -1).astype(jnp.bfloat16), probs, weights)

def attend_back(grad_mixed, query, keys, values, probs, weights):
    grad_mixed, query, keys, values, weights = lax.optimization_barrier((grad_mixed, query, keys, values, weights))
    count = query.shape[0]
    groups = keys.shape[1] // HD
    per_group = query.shape[1] // keys.shape[1]
    q_four = query.astype(jnp.float32).reshape(count, groups, per_group, HD)
    k_three = keys.astype(jnp.float32).reshape(-1, groups, HD)
    v_three = values.astype(jnp.float32).reshape(-1, groups, HD)
    g_four = grad_mixed.astype(jnp.float32).reshape(count, groups, per_group, HD)
    grad_probs = jnp.einsum('igcd,jgd->gcij', g_four, v_three, precision=HIGH)
    grad_values = jnp.einsum('gcij,igcd->jgd', weights.astype(jnp.float32), g_four, precision=HIGH)
    grad_scores = probs * (grad_probs - lax.optimization_barrier(jnp.sum(probs * grad_probs, axis=-1, keepdims=True)))
    scaled = lax.optimization_barrier((grad_scores / math.sqrt(HD)).astype(jnp.bfloat16))
    grad_query = jnp.einsum('gcij,jgd->igcd', scaled.astype(jnp.float32), k_three, precision=HIGH)
    grad_keys = jnp.einsum('gcij,igcd->jgd', scaled.astype(jnp.float32), q_four, precision=HIGH)
    return (grad_query.reshape(count, -1).astype(jnp.bfloat16), grad_keys.reshape(-1, groups * HD), grad_values.reshape(-1, groups * HD))

def slot_entries(slot_rows, gain, w_key, w_value, key_a, key_b, value_a, value_b):
    unit, inverse = normalize(slot_rows)
    slot_normed = lax.optimization_barrier((unit * gain).astype(jnp.bfloat16))
    low_key = mixdot(slot_normed, key_a).astype(jnp.bfloat16)
    low_value = mixdot(slot_normed, value_a).astype(jnp.bfloat16)
    slot_keys = (mixdot(slot_normed, w_key) + mixdot(low_key, key_b)).astype(jnp.bfloat16)
    slot_values = (mixdot(slot_normed, w_value) + mixdot(low_value, value_b)).astype(jnp.bfloat16)
    return (slot_normed, low_key, low_value, slot_keys, slot_values)

def layer_core(rows, slot_rows, params):
    gain, w_query, w_key, w_value, w_out, key_a, key_b, value_a, value_b = params
    unit, inverse = normalize(rows)
    normed = (unit * gain).astype(jnp.bfloat16)
    query = mixdot(normed, w_query).astype(jnp.bfloat16)
    key_tok = mixdot(normed, w_key).astype(jnp.bfloat16)
    value_tok = mixdot(normed, w_value).astype(jnp.bfloat16)
    slot_normed, low_key, low_value, slot_keys, slot_values = slot_entries(slot_rows, gain, w_key, w_value, key_a, key_b, value_a, value_b)
    keys = jnp.concatenate([slot_keys, key_tok], axis=0)
    values = jnp.concatenate([slot_values, value_tok], axis=0)
    mixed, probs, weights = attend(query, keys, values)
    return (unit, inverse, query, keys, values, mixed, probs, weights, slot_normed, low_key, low_value)

def forward(rows, slot_rows, params):
    mixed = layer_core(rows, slot_rows, params)[5]
    return (rows.astype(jnp.float32) + mixdot(mixed, params[4])).astype(jnp.bfloat16)

def backward(rows, slot_rows, grad, params):
    gain, w_query, w_key, w_value, w_out, key_a, key_b, value_a, value_b = params
    unit, inverse, query, keys, values, mixed, probs, weights, slot_normed, low_key, low_value = layer_core(rows, slot_rows, params)
    grad_low = grad.astype(jnp.bfloat16)
    grad_mixed = mixdot(grad_low, w_out.T).astype(jnp.bfloat16)
    grad_query, grad_keys, grad_values = attend_back(grad_mixed, query, keys, values, probs, weights)
    key_grad = grad_keys.astype(jnp.bfloat16)
    value_grad = grad_values.astype(jnp.bfloat16)
    grad_normed = mixdot(grad_query, w_query.T) + mixdot(key_grad[SLOTS:], w_key.T) + mixdot(value_grad[SLOTS:], w_value.T)
    scaled = grad_normed * gain
    grad_rows = grad + inverse * (scaled - unit * lax.optimization_barrier(jnp.mean(scaled * unit, axis=-1, keepdims=True)))
    slot_key_grad = key_grad[:SLOTS]
    slot_value_grad = value_grad[:SLOTS]
    grad_b = jnp.stack([mixdot(low_key.T, slot_key_grad), mixdot(low_value.T, slot_value_grad)])
    low_grads = jnp.stack([mixdot(slot_key_grad, key_b.T), mixdot(slot_value_grad, value_b.T)])
    grad_a = jnp.einsum('sd,tsr->tdr', slot_normed.astype(jnp.float32), low_grads, precision=HIGH)
    return (grad_rows, grad_a, grad_b)

def reference(hidden_in, slot_hidden, norm_gain, w_query, w_key, w_value, w_out, key_a, key_b, value_a, value_b, cotangent):

    def params(layer):
        return (norm_gain[layer], w_query[layer], w_key[layer], w_value[layer], w_out[layer], key_a[layer], key_b[layer], value_a[layer], value_b[layer])

    def one_block(totals, block):
        rows, slot_rows, grad_out = block
        inputs = []
        current = rows
        for layer in range(LAYERS):
            inputs.append(current)
            if layer + 1 < LAYERS:
                current = forward(current, slot_rows[layer], params(layer))
        grad = grad_out.astype(jnp.float32)
        parts_a = [None] * LAYERS
        parts_b = [None] * LAYERS
        for layer in reversed(range(LAYERS)):
            grad, part_a, part_b = backward(inputs[layer], slot_rows[layer], grad, params(layer))
            parts_a[layer] = part_a
            parts_b[layer] = part_b
        return ((totals[0] + jnp.stack(parts_a), totals[1] + jnp.stack(parts_b)), None)
    start = (jnp.zeros((LAYERS, 2, D, RANK), jnp.float32), jnp.zeros((LAYERS, 2, RANK, KVH * HD), jnp.float32))
    slots_by_block = jnp.swapaxes(slot_hidden, 0, 1)
    totals, unused = lax.scan(one_block, start, (hidden_in, slots_by_block, cotangent))
    return (totals[0], totals[1])
```

```python
import functools
import math

import jax
import jax.numpy as jnp
from jax import lax
from jax.experimental import pallas as pl
from jax.experimental.pallas import tpu as pltpu
from jax.sharding import PartitionSpec as P

HD = 128
SLOTS = 16
MICRO = 2
EPS = 1e-05
NEG = -1e30
HIGH = lax.Precision.HIGHEST
SCALE = 1.0 / math.sqrt(HD)
SECTIONS = 4
MP = 4
GROUPS = 2
PER = 3
TILE = 256
TICKS = 2 * SECTIONS + MICRO - 2


F32 = jnp.float32
BF16 = jnp.bfloat16
ANY = pl.BlockSpec(memory_space=pl.ANY)
VMEM = pl.BlockSpec(memory_space=pltpu.VMEM)
SMEM = pl.BlockSpec(memory_space=pltpu.SMEM)


def mixdot(left, right):
    return jnp.dot(left, right, preferred_element_type=F32)


def dot_nt(left, right):
    return lax.dot_general(left, right, (((1,), (1,)), ((), ())), preferred_element_type=F32)


def dot_tn(left, right):
    return lax.dot_general(left, right, (((0,), (0,)), ((), ())), preferred_element_type=F32)


def in_flight(index):
    return (index >= 0) & (index < MICRO)


def probabilities(q_three, keys, count):
    scores = dot_nt(q_three, keys) * SCALE
    row = lax.broadcasted_iota(jnp.int32, scores.shape, 0) % count
    col = lax.broadcasted_iota(jnp.int32, scores.shape, 1)
    seen = (col <= row) | ((col >= count) & (col < count + SLOTS))
    scores = jnp.where(seen, scores, NEG)
    top = jnp.max(scores, axis=-1, keepdims=True)
    raised = jnp.exp(scores - top)
    return raised / jnp.sum(raised, axis=-1, keepdims=True)


def tick_kernel(tick, count, *refs):
    has_pieces = tick > 0
    may_f = tick <= SECTIONS - 2 + MICRO - 1
    may_p = SECTIONS - 1 <= tick <= SECTIONS - 1 + MICRO - 1
    may_b = tick >= SECTIONS - 1
    refs = list(refs)
    info, hidden, cot = refs[:3]
    del refs[:3]
    pieces = refs[:MP] if has_pieces else []
    del refs[: len(pieces)]
    gain, slot_kv, wq, wk, wv, wo = refs[:6]
    del refs[:6]
    carried = 0 if tick == 0 else (2 if tick <= SECTIONS - 1 else 3)
    del refs[:carried]
    part, kept_qkv, kept_own = refs[:3]
    del refs[:3]
    kept_slot = None
    if may_b:
        kept_slot = refs.pop(0)
    (xbuf, gbuf, normed, qkv, w_all, w_o, mixed, gtile, sgrad, wsem, isem, osem) = refs

    section = info[0]
    me = info[1]
    share = count // MP
    b_f = tick - section
    b_b = tick - (2 * SECTIONS - 2) + section
    last = section == SECTIONS - 1
    do_f = in_flight(b_f) & jnp.logical_not(last) if may_f else None
    do_p = in_flight(b_f) & last if may_p else None
    do_b = in_flight(b_b) if may_b else None

    def weight_copy(j):
        source = wq.at[0, :, pl.ds(j * TILE, TILE)] if j < 3 else (wk, wv)[j - 3].at[0]
        return pltpu.make_async_copy(source, w_all.at[j], wsem.at[j])

    def out_copy(j):
        rows = pl.ds(j * TILE, TILE)
        return pltpu.make_async_copy(wo.at[0, rows], w_o.at[rows], wsem.at[5 + j])

    def piece_copies(target, base):
        found = []
        for offset in range(MP):
            place = pl.multiple_of(lax.rem(me + MP - offset, MP) * share, share)
            found.append(
                pltpu.make_async_copy(
                    pieces[offset], target.at[pl.ds(place, share)], isem.at[base + offset]
                )
            )
        return found

    def qkv_weights_start():
        for j in range(5):
            weight_copy(j).start()

    def out_weights_start():
        for j in range(3):
            out_copy(j).start()

    def project():
        def norm_rows(i, carry):
            rows = pl.ds(pl.multiple_of(i * 16, 16), 16)
            wide = xbuf[rows].astype(F32)
            inverse = lax.rsqrt(jnp.mean(wide * wide, axis=-1, keepdims=True) + EPS)
            normed[rows] = (wide * inverse * gain[...]).astype(BF16)
            return carry

        lax.fori_loop(0, count // 16, norm_rows, 0)

        for j in range(5):
            weight_copy(j).wait()
            qkv[j] = mixdot(normed[...], w_all[j]).astype(BF16)

    def group_operands(group, block):
        cols = slice(group * HD, (group + 1) * HD)
        parts = []
        for head in range(group * PER, (group + 1) * PER):
            parts.append(qkv[head // 2, :, (head % 2) * HD : (head % 2 + 1) * HD])
        q_three = jnp.concatenate(parts, axis=0)
        pad = jnp.zeros((TILE - count - SLOTS, HD), BF16)
        keys = jnp.concatenate([qkv[3, :, cols], slot_kv[block, 0, :, cols], pad], axis=0)
        values = jnp.concatenate([qkv[4, :, cols], slot_kv[block, 1, :, cols], pad], axis=0)
        return q_three, keys, values

    def load_rows(block):
        if tick <= MICRO - 1:

            @pl.when(section == 0)
            def _():
                copy = pltpu.make_async_copy(hidden.at[block], xbuf, isem.at[0])
                copy.start()

        if has_pieces:

            @pl.when(section > 0)
            def _():
                for copy in piece_copies(xbuf, 0):
                    copy.start()

    def wait_rows(block):
        if tick <= MICRO - 1:

            @pl.when(section == 0)
            def _():
                pltpu.make_async_copy(hidden.at[block], xbuf, isem.at[0]).wait()

        if has_pieces:

            @pl.when(section > 0)
            def _():
                for copy in piece_copies(xbuf, 0):
                    copy.wait()

    def keep_copies(block):
        place = pl.multiple_of(me * share, share)
        return (
            pltpu.make_async_copy(qkv, kept_qkv.at[block], osem.at[0]),
            pltpu.make_async_copy(xbuf.at[pl.ds(place, share)], kept_own.at[block], osem.at[1]),
        )

    def forward(block, full):
        load_rows(block)
        qkv_weights_start()
        out_weights_start()
        if not full:
            pltpu.make_async_copy(cot.at[block], gbuf, isem.at[4]).start()
        wait_rows(block)
        project()
        for copy in keep_copies(block):
            copy.start()
        if full:
            for group in range(GROUPS):
                q_three, keys, values = group_operands(group, block)
                probs = probabilities(q_three, keys, count)
                heads = mixdot(probs.astype(BF16), values).astype(BF16)
                for k in range(PER):
                    head = group * PER + k
                    mixed[:, head * HD : (head + 1) * HD] = heads[k * count : (k + 1) * count]
            for j in range(3):
                out_copy(j).wait()

            def out_tile(n, carry):
                cols = pl.ds(pl.multiple_of(n * 512, 512), 512)
                part[:, cols] = mixdot(mixed[...], w_o[:, cols]).astype(BF16)
                return carry

            lax.fori_loop(0, part.shape[1] // 512, out_tile, 0)
        for copy in keep_copies(block):
            copy.wait()

    if may_f:

        @pl.when(do_f)
        def _():
            forward(b_f, True)

    if may_p:

        @pl.when(do_p)
        def _():
            forward(b_f, False)

    if may_b:

        @pl.when(do_b & jnp.logical_not(last))
        def _():
            for copy in piece_copies(gbuf, 0):
                copy.start()
            out_weights_start()
            pltpu.make_async_copy(kept_qkv.at[b_b], qkv, isem.at[5]).start()

            @pl.when(section > 0)
            def _():
                qkv_weights_start()

            for copy in piece_copies(gbuf, 0):
                copy.wait()
            pltpu.make_async_copy(kept_qkv.at[b_b], qkv, isem.at[5]).wait()

        @pl.when(do_b)
        def _():
            @pl.when(last)
            def _():
                pltpu.make_async_copy(cot.at[b_b], gbuf, isem.at[4]).wait()

            for j in range(3):
                out_copy(j).wait()
                rows = slice(j * TILE, (j + 1) * TILE)
                mixed[:, rows] = dot_nt(gbuf[...], w_o[rows]).astype(BF16)
            for group in range(GROUPS):
                q_three, keys, values = group_operands(group, b_b)
                probs = probabilities(q_three, keys, count)
                g_three = jnp.concatenate(
                    [
                        mixed[:, (group * PER + k) * HD : (group * PER + k + 1) * HD]
                        for k in range(PER)
                    ],
                    axis=0,
                )
                grad_probs = dot_nt(g_three, values)
                grad_values = dot_tn(probs.astype(BF16), g_three).astype(BF16)
                centre = jnp.sum(probs * grad_probs, axis=-1, keepdims=True)
                scaled = (probs * (grad_probs - centre) * SCALE).astype(BF16)
                grad_query = mixdot(scaled, keys).astype(BF16)
                grad_keys = dot_tn(scaled, q_three).astype(BF16)
                for k in range(PER):
                    head = group * PER + k
                    half = slice((head % 2) * HD, (head % 2 + 1) * HD)
                    gtile[head // 2, :, half] = grad_query[k * count : (k + 1) * count]
                cols = slice(group * HD, (group + 1) * HD)
                gtile[3, :, cols] = grad_keys[:count]
                gtile[4, :, cols] = grad_values[:count]
                sgrad[0, :, cols] = grad_keys[count : count + SLOTS]
                sgrad[1, :, cols] = grad_values[count : count + SLOTS]
            pltpu.make_async_copy(sgrad, kept_slot.at[b_b], osem.at[2]).start()

            @pl.when(section > 0)
            def _():
                @pl.when(jnp.logical_not(last))
                def _():
                    for j in range(5):
                        weight_copy(j).wait()

                def in_tile(n, carry):
                    cols = pl.ds(pl.multiple_of(n * 512, 512), 512)
                    total = dot_nt(gtile[0], w_all[0, cols])
                    for j in range(1, 5):
                        total = total + dot_nt(gtile[j], w_all[j, cols])
                    part[:, cols] = total.astype(BF16)
                    return carry

                lax.fori_loop(0, part.shape[1] // 512, in_tile, 0)

            pltpu.make_async_copy(sgrad, kept_slot.at[b_b], osem.at[2]).wait()


def run_tick(tick, info, hidden, cot, pieces, gain, slot_kv, wq, wk, wv, wo, kept):
    count, width = hidden.shape[1:]
    share = count // MP
    heads = wq.shape[2]
    keep = [
        jax.ShapeDtypeStruct((MICRO, 5, count, TILE), BF16),
        jax.ShapeDtypeStruct((MICRO, share, width), BF16),
    ]
    if tick >= SECTIONS - 1:
        keep.append(jax.ShapeDtypeStruct((MICRO, 2, SLOTS, TILE), BF16))
    first_kept = 9 + len(pieces)
    return pl.pallas_call(
        functools.partial(tick_kernel, tick, count),
        out_shape=[jax.ShapeDtypeStruct((count, width), BF16)] + keep,
        in_specs=[SMEM, ANY, ANY] + [ANY] * len(pieces) + [VMEM, VMEM] + [ANY] * (4 + len(kept)),
        out_specs=[VMEM] + [ANY] * len(keep),
        scratch_shapes=[
            pltpu.VMEM((count, width), BF16),
            pltpu.VMEM((count, width), BF16),
            pltpu.VMEM((count, width), BF16),
            pltpu.VMEM((5, count, TILE), BF16),
            pltpu.VMEM((5, width, TILE), BF16),
            pltpu.VMEM((heads, width), BF16),
            pltpu.VMEM((count, heads), BF16),
            pltpu.VMEM((5, count, TILE), BF16),
            pltpu.VMEM((2, SLOTS, TILE), BF16),
            pltpu.SemaphoreType.DMA((8,)),
            pltpu.SemaphoreType.DMA((6,)),
            pltpu.SemaphoreType.DMA((3,)),
        ],
        input_output_aliases={first_kept + i: 1 + i for i in range(len(kept))},
        compiler_params=pltpu.CompilerParams(vmem_limit_bytes=40 << 20),
        name=f"tick{tick}",
    )(info, hidden, cot, *pieces, gain, slot_kv, wq, wk, wv, wo, *kept)


def update_kernel(tick, share, info, arrived, gain, own, cot, piece, out, xbuf, gbuf, sem):
    may_f = tick <= SECTIONS - 2 + MICRO - 1
    may_b = tick >= SECTIONS - 1
    section = info[0]
    me = info[1]
    b_f = tick - section
    b_b = tick - (2 * SECTIONS - 2) + section
    last = section == SECTIONS - 1

    def summed(rows):
        total = arrived[0, rows].astype(F32)
        for k in range(1, MP):
            total = total + arrived[k, rows].astype(F32)
        return total

    if may_f:

        @pl.when(in_flight(b_f) & jnp.logical_not(last))
        def _():
            copy = pltpu.make_async_copy(own.at[b_f], xbuf, sem.at[0])
            copy.start()
            copy.wait()

            def rows_of(i, carry):
                rows = pl.ds(pl.multiple_of(i * 16, 16), 16)
                out[rows] = (xbuf[rows].astype(F32) + summed(rows)).astype(BF16)
                return carry

            lax.fori_loop(0, share // 16, rows_of, 0)

    if may_b:

        @pl.when(in_flight(b_b) & (section > 0))
        def _():
            copy = pltpu.make_async_copy(own.at[b_b], xbuf, sem.at[0])
            copy.start()

            @pl.when(last)
            def _():
                place = pl.multiple_of(me * share, share)
                pltpu.make_async_copy(cot.at[b_b, pl.ds(place, share)], gbuf, sem.at[1]).start()

            @pl.when(jnp.logical_not(last))
            def _():
                pltpu.make_async_copy(piece, gbuf, sem.at[1]).start()

            copy.wait()

            @pl.when(last)
            def _():
                place = pl.multiple_of(me * share, share)
                pltpu.make_async_copy(cot.at[b_b, pl.ds(place, share)], gbuf, sem.at[1]).wait()

            @pl.when(jnp.logical_not(last))
            def _():
                pltpu.make_async_copy(piece, gbuf, sem.at[1]).wait()

            def rows_of(i, carry):
                rows = pl.ds(pl.multiple_of(i * 16, 16), 16)
                wide = xbuf[rows].astype(F32)
                inverse = lax.rsqrt(jnp.mean(wide * wide, axis=-1, keepdims=True) + EPS)
                unit = wide * inverse
                scaled = summed(rows) * gain[...]
                centre = jnp.mean(scaled * unit, axis=-1, keepdims=True)
                change = inverse * (scaled - unit * centre)
                out[rows] = (gbuf[rows].astype(F32) + change).astype(BF16)
                return carry

            lax.fori_loop(0, share // 16, rows_of, 0)


def run_update(tick, info, arrived, gain, own, cot, piece):
    share, width = arrived.shape[1:]
    return pl.pallas_call(
        functools.partial(update_kernel, tick, share),
        out_shape=jax.ShapeDtypeStruct((share, width), BF16),
        in_specs=[SMEM, VMEM, VMEM, ANY, ANY, ANY],
        out_specs=VMEM,
        scratch_shapes=[
            pltpu.VMEM((share, width), BF16),
            pltpu.VMEM((share, width), BF16),
            pltpu.SemaphoreType.DMA((2,)),
        ],
        compiler_params=pltpu.CompilerParams(vmem_limit_bytes=16 << 20),
        name=f"update{tick}",
    )(info, arrived, gain, own, cot, piece)


def routes(tick, offset):
    pairs = []
    for section in range(SECTIONS):
        target = None
        if section < SECTIONS - 1 and 0 <= tick - section < MICRO:
            target = section + 1
        if section > 0 and 0 <= tick - (2 * SECTIONS - 2) + section < MICRO:
            target = section - 1
        if target is not None:
            for m in range(MP):
                pairs.append((section * MP + m, target * MP + (m + offset) % MP))
    return pairs


def copy_for_each(array, axis):
    copies = jnp.broadcast_to(array, (lax.axis_size(axis), *array.shape))
    return lax.all_to_all(copies, axis, split_axis=0, concat_axis=0, tiled=True)


def normalize(rows):
    wide = rows.astype(F32)
    return wide * lax.rsqrt(jnp.mean(wide * wide, axis=-1, keepdims=True) + EPS)


def local(
    hidden_in,
    slot_hidden,
    norm_gain,
    w_query,
    w_key,
    w_value,
    w_out,
    key_a,
    key_b,
    value_a,
    value_b,
    cotangent,
):
    width = hidden_in.shape[2]
    share = hidden_in.shape[1] // MP
    info = jnp.stack([lax.axis_index("section"), lax.axis_index("mp")]).astype(jnp.int32)

    slot_normed = (normalize(slot_hidden[0]) * norm_gain[0]).astype(BF16)
    slot_rows = slot_normed.reshape(-1, width)
    low_key = mixdot(slot_rows, key_a[0]).astype(BF16)
    low_value = mixdot(slot_rows, value_a[0]).astype(BF16)
    slot_keys = mixdot(slot_rows, w_key[0]) + mixdot(low_key, key_b[0])
    slot_values = mixdot(slot_rows, w_value[0]) + mixdot(low_value, value_b[0])
    slot_kv = jnp.stack([slot_keys, slot_values]).astype(BF16)
    slot_kv = jnp.swapaxes(slot_kv.reshape(2, MICRO, SLOTS, -1), 0, 1)

    all_slots = copy_for_each(slot_rows, "dp").reshape(-1, width)

    pieces = []
    kept = []
    for tick in range(TICKS):
        part, *kept = run_tick(
            tick,
            info,
            hidden_in,
            cotangent,
            pieces,
            norm_gain,
            slot_kv,
            w_query,
            w_key,
            w_value,
            w_out,
            kept,
        )
        if tick + 1 < TICKS:
            arrived = lax.all_to_all(part.reshape(MP, share, width), "mp", 0, 0, tiled=True)
            own_piece = pieces[0] if pieces else arrived[0]
            send = run_update(tick, info, arrived, norm_gain, kept[1], cotangent, own_piece)
            pieces = [
                lax.ppermute(send, ("section", "mp"), routes(tick, offset)) for offset in range(MP)
            ]

    slot_grads = kept[2]
    all_grads = copy_for_each(slot_grads, "dp")
    all_grads = jnp.moveaxis(all_grads.reshape(-1, 2, SLOTS, TILE), 1, 0).reshape(2, -1, TILE)
    grad_k, grad_v = all_grads[0], all_grads[1]
    lows = jnp.concatenate(
        [
            lax.dot_general(grad_k, key_b[0], (((1,), (1,)), ((), ())), preferred_element_type=F32),
            lax.dot_general(
                grad_v, value_b[0], (((1,), (1,)), ((), ())), preferred_element_type=F32
            ),
        ],
        axis=1,
    )
    low_total = jnp.sum(copy_for_each(lows, "mp"), axis=0)
    term = lax.dot_general(
        all_slots.astype(F32), low_total, (((0,), (0,)), ((), ())), precision=HIGH
    )
    rank = key_a.shape[2]
    grad_a = jnp.stack([term[:, :rank], term[:, rank:]])
    all_low_key = mixdot(all_slots, key_a[0]).astype(BF16)
    all_low_value = mixdot(all_slots, value_a[0]).astype(BF16)
    grad_b = jnp.stack([dot_tn(all_low_key, grad_k), dot_tn(all_low_value, grad_v)])
    return (grad_a[None], grad_b[None])


def solution(mesh):
    placed = (
        P("dp", None, None),
        P("section", "dp", None, None),
        P("section", None),
        P("section", None, "mp"),
        P("section", None, "mp"),
        P("section", None, "mp"),
        P("section", "mp", None),
        P("section", None, None),
        P("section", None, "mp"),
        P("section", None, None),
        P("section", None, "mp"),
        P("dp", None, None),
    )
    return jax.shard_map(
        local,
        mesh=mesh,
        in_specs=placed,
        out_specs=(P("section", None, None, None), P("section", None, None, "mp")),
        check_vma=False,
    )
```

```python
import functools
import math

import jax
import jax.numpy as jnp
from jax import lax
from jax.experimental import pallas as pl
from jax.experimental.pallas import tpu as pltpu
from jax.sharding import PartitionSpec as P

HD = 128
SLOTS = 16
MICRO = 2
EPS = 1e-05
NEG = -1e30
HIGH = lax.Precision.HIGHEST
SCALE = 1.0 / math.sqrt(HD)
SECTIONS = 4
MP = 4
GROUPS = 2
PER = 3
TILE = 256
TICKS = 2 * SECTIONS + MICRO - 2


F32 = jnp.float32
BF16 = jnp.bfloat16
VMEM = pl.BlockSpec(memory_space=pltpu.VMEM)
HBM = pl.BlockSpec(memory_space=pltpu.HBM)
VMEM_FIRST = 24 << 20
VMEM_TICK = 12 << 20
VMEM_END = 16 << 20
VMEM_UPDATE = 4 << 20
SMEM = pl.BlockSpec(memory_space=pltpu.SMEM)


def mixdot(left, right):
    return jnp.dot(left, right, preferred_element_type=F32)


def dot_nt(left, right):
    return lax.dot_general(left, right, (((1,), (1,)), ((), ())), preferred_element_type=F32)


def dot_tn(left, right):
    return lax.dot_general(left, right, (((0,), (0,)), ((), ())), preferred_element_type=F32)


def in_flight(index):
    return (index >= 0) & (index < MICRO)


def probabilities(q_three, keys, count):
    scores = dot_nt(q_three, keys) * SCALE
    row = lax.broadcasted_iota(jnp.int32, scores.shape, 0) % count
    col = lax.broadcasted_iota(jnp.int32, scores.shape, 1)
    seen = (col <= row) | ((col >= count) & (col < count + SLOTS))
    scores = jnp.where(seen, scores, NEG)
    top = jnp.max(scores, axis=-1, keepdims=True)
    raised = jnp.exp(scores - top)
    return raised / jnp.sum(raised, axis=-1, keepdims=True)


def slot_rounds(tick):
    table = {0: (2, 3, 4), 1: (0, 3, 4), 2: (0, 1, 6), 3: (0, 1, 2)}
    return [(s, ticks.index(tick)) for s, ticks in table.items() if tick in ticks]


def other_half(place):
    return jnp.where(place < 4, place + 4, place - 4)


def slot_source(place, number):
    return place if number < 2 else other_half(place)


def slot_members(place, number, k):
    if number == 0:
        return 2 * k + place % 2
    return jnp.where(place < 4, 0, 4) + k


def tick_kernel(tick, count, *refs):
    has_pieces = tick > 0
    may_f = tick <= SECTIONS - 2 + MICRO - 1
    may_p = SECTIONS - 1 <= tick <= SECTIONS - 1 + MICRO - 1
    may_b = tick >= SECTIONS - 1
    refs = list(refs)
    take = lambda n: [refs.pop(0) for _ in range(n)]
    info, gain = take(2)
    wq = wk = wv = hidden = late = None
    if tick == 0:
        hbm = [gain] + take(10)
        gain, late, wk, wv, wq, wo, slot_kv, slots = take(8)
    elif tick < TICKS - 1:
        slot_kv, wo, slots, wq, wk, wv = take(6)
    else:
        slot_kv, wo = take(2)
    late = take(1)[0] if 0 < tick < MICRO else late
    cot = take(1)[0] if may_p else None
    pieces = take(MP) if has_pieces else []
    take(kept_before(tick))
    part, kept_qkv, kept_own = take(3)
    kept_slot = take(1)[0] if may_b else None
    ends = take(1)[0] if tick == TICKS - 1 else None
    normed, gbuf, mixed, gtile, *first = refs

    section = info[0]
    me = info[1]
    share = count // MP
    width = part.shape[1]
    b_f = tick - section
    b_b = tick - (2 * SECTIONS - 2) + section
    last = section == SECTIONS - 1
    do_b = in_flight(b_b) if may_b else None

    copies = []
    if tick == 0:
        g_hbm, h_hbm, wk_hbm, wv_hbm, wq_hbm, wo_hbm, *slot_hbm = hbm
        slot_rows, key_a, key_b, value_a, value_b, sems = first
        pairs = [(g_hbm, gain)]
        pairs += list(zip(slot_hbm, (slot_rows, key_a, key_b, value_a, value_b)))
        pairs += [(wk_hbm, wk), (wv_hbm, wv), (h_hbm.at[0], gbuf)]
        for j in range(3):
            cols = pl.ds(j * TILE, TILE)
            pairs.append((wq_hbm.at[0, :, cols], wq.at[0, :, cols]))
        pairs += [(wo_hbm, wo), (h_hbm.at[1], late)]
        copies = [
            pltpu.make_async_copy(source, target, sems.at[i])
            for i, (source, target) in enumerate(pairs)
        ]
        hidden = gbuf
        for copy in copies:
            copy.start()

    def columns(j):
        if j < 3:
            return wq.at[0, :, pl.ds(j * TILE, TILE)]
        return (wk, wv)[j - 3].at[0]

    def normalize_into(source, place, rows, to=None):
        to = normed if to is None else to

        def some(i, carry):
            part_rows = pl.ds(pl.multiple_of(i * 16, 16), 16)
            wide = source[part_rows].astype(F32)
            inverse = lax.rsqrt(jnp.mean(wide * wide, axis=-1, keepdims=True) + EPS)
            target = pl.ds(pl.multiple_of(place + i * 16, 16), 16)
            to[target] = (wide * inverse * gain[...]).astype(BF16)
            return carry

        lax.fori_loop(0, rows // 16, some, 0)

    def place_of(offset):
        return pl.multiple_of(lax.rem(me + MP - offset, MP) * share, share)

    def project(block):
        if tick < MICRO:
            rows = hidden if tick == 0 else late

            @pl.when(section == 0)
            def _():
                normalize_into(rows, 0, count)
                kept_own[block] = rows[pl.ds(place_of(0), share)]

        if has_pieces:

            @pl.when(section > 0)
            def _():
                for offset in range(MP):
                    normalize_into(pieces[offset], place_of(offset), share)
                kept_own[block] = pieces[0][...]

        for j in (3, 4, 0, 1, 2):
            if tick == 0 and j < 3:
                copies[9 + j].wait()
            kept_qkv[block, j] = mixdot(normed[...], columns(j)[...]).astype(BF16)

    def group_operands(group, block):
        cols = slice(group * HD, (group + 1) * HD)
        parts = []
        for head in range(group * PER, (group + 1) * PER):
            parts.append(kept_qkv[block, head // 2, :, (head % 2) * HD : (head % 2 + 1) * HD])
        q_three = jnp.concatenate(parts, axis=0)
        pad = jnp.zeros((TILE - count - SLOTS, HD), BF16)
        keys = jnp.concatenate([kept_qkv[block, 3, :, cols], slot_kv[block, 0, :, cols], pad], axis=0)
        values = jnp.concatenate(
            [kept_qkv[block, 4, :, cols], slot_kv[block, 1, :, cols], pad], axis=0
        )
        return q_three, keys, values

    if tick == 0:
        for copy in copies[:2]:
            copy.wait()
        own_slots = pl.ds(pl.multiple_of(info[2] * MICRO * SLOTS, MICRO * SLOTS), MICRO * SLOTS)
        slot_normed = slots.at[own_slots]
        normalize_into(slot_rows, 0, MICRO * SLOTS, slot_normed)
        for copy in copies[2:9]:
            copy.wait()
        low_key = dot_nt(slot_normed[...], key_a[...]).astype(BF16)
        low_value = dot_nt(slot_normed[...], value_a[...]).astype(BF16)
        slot_keys = mixdot(slot_normed[...], wk[0]) + mixdot(low_key, key_b[...])
        slot_values = mixdot(slot_normed[...], wv[0]) + mixdot(low_value, value_b[...])
        for block in range(MICRO):
            rows = slice(block * SLOTS, (block + 1) * SLOTS)
            slot_kv[block, 0] = slot_keys[rows].astype(BF16)
            slot_kv[block, 1] = slot_values[rows].astype(BF16)

        @pl.when(section > 0)
        def _():
            for copy in copies[9:]:
                copy.wait()

    if tick < TICKS - 1:
        for spare, number in slot_rounds(tick):

            @pl.when(section == spare)
            def _():
                source = slot_source(info[2], number)
                for k in range(MP):
                    rows = pl.ds(pl.multiple_of(source * share, share), share)
                    part[k * share : (k + 1) * share] = slots[rows]

    if may_f:

        @pl.when(in_flight(b_f) & jnp.logical_not(last))
        def _():
            project(b_f)
            for group in range(GROUPS):
                q_three, keys, values = group_operands(group, b_f)
                probs = probabilities(q_three, keys, count)
                heads = mixdot(probs.astype(BF16), values).astype(BF16)
                for k in range(PER):
                    head = group * PER + k
                    mixed[:, head * HD : (head + 1) * HD] = heads[k * count : (k + 1) * count]

            for copy in copies[12:]:
                copy.wait()

            def out_tile(n, carry):
                cols = pl.ds(pl.multiple_of(n * 512, 512), 512)
                part[:, cols] = mixdot(mixed[...], wo[0, :, cols]).astype(BF16)
                return carry

            lax.fori_loop(0, width // 512, out_tile, 0)

    if may_p:

        @pl.when(in_flight(b_f) & last)
        def _():
            project(b_f)
            gbuf[...] = cot[b_f]

    if may_b:
        if tick > SECTIONS - 1:

            @pl.when(do_b & jnp.logical_not(last))
            def _():
                for offset in range(MP):
                    gbuf[pl.ds(place_of(offset), share)] = pieces[offset][...]

        @pl.when(do_b)
        def _():
            for j in range(3):
                rows = slice(j * TILE, (j + 1) * TILE)
                mixed[:, rows] = dot_nt(gbuf[...], wo[0, rows]).astype(BF16)
            for group in range(GROUPS):
                q_three, keys, values = group_operands(group, b_b)
                probs = probabilities(q_three, keys, count)
                g_three = jnp.concatenate(
                    [
                        mixed[:, (group * PER + k) * HD : (group * PER + k + 1) * HD]
                        for k in range(PER)
                    ],
                    axis=0,
                )
                grad_probs = dot_nt(g_three, values)
                grad_values = dot_tn(probs.astype(BF16), g_three).astype(BF16)
                centre = jnp.sum(probs * grad_probs, axis=-1, keepdims=True)
                scaled = (probs * (grad_probs - centre) * SCALE).astype(BF16)
                grad_query = mixdot(scaled, keys).astype(BF16)
                grad_keys = dot_tn(scaled, q_three).astype(BF16)
                for k in range(PER):
                    head = group * PER + k
                    half = slice((head % 2) * HD, (head % 2 + 1) * HD)
                    gtile[head // 2, :, half] = grad_query[k * count : (k + 1) * count]
                cols = slice(group * HD, (group + 1) * HD)
                gtile[3, :, cols] = grad_keys[:count]
                gtile[4, :, cols] = grad_values[:count]
                kept_slot[b_b, 0, :, cols] = grad_keys[count : count + SLOTS]
                kept_slot[b_b, 1, :, cols] = grad_values[count : count + SLOTS]

        if tick == TICKS - 1:
            for d in range(ends.shape[0]):
                ends[d] = kept_slot[...]

        if tick < TICKS - 1:

            @pl.when(do_b & (section > 0))
            def _():
                def in_tile(n, carry):
                    cols = pl.ds(pl.multiple_of(n * 512, 512), 512)
                    total = dot_nt(gtile[0], columns(0)[cols])
                    for j in range(1, 5):
                        total = total + dot_nt(gtile[j], columns(j)[cols])
                    part[:, cols] = total.astype(BF16)
                    return carry

                lax.fori_loop(0, width // 512, in_tile, 0)


def kept_before(tick):
    return 0 if tick == 0 else (2 if tick <= SECTIONS - 1 else 3)


def run_tick(tick, info, gain, operands, shapes, pieces, kept):
    count, width, heads = shapes["sizes"]
    share = count // MP
    keep = [
        jax.ShapeDtypeStruct((MICRO, 5, count, TILE), BF16),
        jax.ShapeDtypeStruct((MICRO, share, width), BF16),
    ]
    if tick >= SECTIONS - 1:
        keep.append(jax.ShapeDtypeStruct((MICRO, 2, SLOTS, TILE), BF16))
    ends = []
    if tick == TICKS - 1:
        ends.append(jax.ShapeDtypeStruct((shapes["parts"], *keep[2].shape), BF16))
    operands = operands + list(pieces)
    first_kept = 2 + len(operands)
    given = shapes["given"] if tick == 0 else []
    in_specs = [SMEM] + [VMEM] * (1 + len(operands) + len(kept))
    if tick == 0:
        in_specs[1:] = [HBM] * 11
    scratch = [
        pltpu.VMEM((count, width), BF16),
        pltpu.VMEM((count, width), BF16),
        pltpu.VMEM((count, heads), BF16),
        pltpu.VMEM((5, count, TILE), BF16),
    ]
    if tick == 0:
        scratch += [pltpu.VMEM(array.shape, BF16) for array in operands[5:]]
        scratch.append(pltpu.SemaphoreType.DMA((14,)))
    return pl.pallas_call(
        functools.partial(tick_kernel, tick, count),
        out_shape=given + [jax.ShapeDtypeStruct((count, width), BF16)] + keep + ends,
        in_specs=in_specs,
        out_specs=[VMEM] * (len(given) + 1 + len(keep) + len(ends)),
        scratch_shapes=scratch,
        input_output_aliases={first_kept + i: 1 + i for i in range(len(kept))},
        compiler_params=pltpu.CompilerParams(
            vmem_limit_bytes=VMEM_FIRST if tick == 0 else VMEM_TICK
        ),
        name=f"tick{tick}",
    )(info, gain, *operands, *kept)


def update_kernel(tick, share, *refs):
    may_f = tick <= SECTIONS - 2 + MICRO - 1
    may_b = tick >= SECTIONS - 1
    may_p = SECTIONS - 1 <= tick <= SECTIONS - 1 + MICRO - 1
    refs = list(refs)
    info, arrived, gain, own = refs[:4]
    del refs[:4]
    cot = refs.pop(0) if may_p else None
    piece = refs.pop(0) if may_b else None
    _, out, slots = refs
    section = info[0]
    me = info[1]
    b_f = tick - section
    b_b = tick - (2 * SECTIONS - 2) + section
    last = section == SECTIONS - 1

    for spare, number in slot_rounds(tick):

        @pl.when(section == spare)
        def _():
            for k in range(MP):
                source = slot_source(slot_members(info[2], number, k), number)
                slots[pl.ds(pl.multiple_of(source * share, share), share)] = arrived[k]

    def summed(rows):
        total = arrived[0, rows].astype(F32)
        for k in range(1, MP):
            total = total + arrived[k, rows].astype(F32)
        return total

    def step_back(grad_of):
        def rows_of(i, carry):
            rows = pl.ds(pl.multiple_of(i * 16, 16), 16)
            wide = own[b_b, rows].astype(F32)
            inverse = lax.rsqrt(jnp.mean(wide * wide, axis=-1, keepdims=True) + EPS)
            unit = wide * inverse
            scaled = summed(rows) * gain[...]
            centre = jnp.mean(scaled * unit, axis=-1, keepdims=True)
            change = inverse * (scaled - unit * centre)
            out[rows] = (grad_of(i, rows).astype(F32) + change).astype(BF16)
            return carry

        lax.fori_loop(0, share // 16, rows_of, 0)

    if may_f:

        @pl.when(in_flight(b_f) & jnp.logical_not(last))
        def _():
            def rows_of(i, carry):
                rows = pl.ds(pl.multiple_of(i * 16, 16), 16)
                out[rows] = (own[b_f, rows].astype(F32) + summed(rows)).astype(BF16)
                return carry

            lax.fori_loop(0, share // 16, rows_of, 0)

    if may_p:

        @pl.when(in_flight(b_b) & last)
        def _():
            step_back(lambda i, rows: cot[b_b, pl.ds(pl.multiple_of(me * share + i * 16, 16), 16)])

    if may_b and tick > SECTIONS - 1:

        @pl.when(in_flight(b_b) & (section > 0) & jnp.logical_not(last))
        def _():
            step_back(lambda i, rows: piece[rows])


def run_update(tick, info, arrived, gain, own, cot, piece, slots):
    share, width = arrived.shape[1:]
    operands = [arrived, gain, own]
    if SECTIONS - 1 <= tick <= SECTIONS - 1 + MICRO - 1:
        operands.append(cot)
    if tick >= SECTIONS - 1:
        operands.append(piece)
    operands.append(slots)
    return pl.pallas_call(
        functools.partial(update_kernel, tick, share),
        out_shape=[
            jax.ShapeDtypeStruct((share, width), BF16),
            jax.ShapeDtypeStruct(slots.shape, BF16),
        ],
        in_specs=[SMEM] + [VMEM] * len(operands),
        out_specs=[VMEM] * 2,
        input_output_aliases={len(operands): 1},
        compiler_params=pltpu.CompilerParams(vmem_limit_bytes=VMEM_UPDATE),
        name=f"update{tick}",
    )(info, *operands)


def routes(tick, offset):
    pairs = []
    for section in range(SECTIONS):
        target = None
        if section < SECTIONS - 1 and 0 <= tick - section < MICRO:
            target = section + 1
        if section > 0 and 0 <= tick - (2 * SECTIONS - 2) + section < MICRO:
            target = section - 1
        if target is not None:
            for m in range(MP):
                pairs.append((section * MP + m, target * MP + (m + offset) % MP))
    return pairs


def sum_groups(tick, parts):
    found = []
    for section in range(SECTIONS):
        forward = section < SECTIONS - 1 and 0 <= tick - section < MICRO
        backward = section > 0 and 0 <= tick - (2 * SECTIONS - 2) + section < MICRO
        place = lambda d, m: (d * SECTIONS + section) * MP + m
        if forward or backward:
            found += [[place(d, m) for m in range(MP)] for d in range(parts)]
            continue
        if dict(slot_rounds(tick)).get(section, 0) == 0:
            sets = [[2 * k + low for k in range(MP)] for low in range(2)]
        else:
            sets = [[4 * high + k for k in range(MP)] for high in range(2)]
        found += [[place(d, m) for d in members] for members in sets for m in range(MP)]
    return found


def grads_of(grads, kind):
    blocks = [grads[d, block, kind] for d in range(grads.shape[0]) for block in range(MICRO)]
    return jnp.concatenate(blocks, axis=0)


def lows_kernel(grads, key_b, value_b, out):
    low_key = dot_nt(grads_of(grads, 0), key_b[...])
    low_value = dot_nt(grads_of(grads, 1), value_b[...])
    total = jnp.concatenate([low_key, low_value], axis=1)
    for k in range(MP):
        out[k] = total


def run_lows(grads, key_b, value_b):
    rows = grads.shape[0] * MICRO * SLOTS
    return pl.pallas_call(
        lows_kernel,
        out_shape=jax.ShapeDtypeStruct((MP, rows, 2 * key_b.shape[0]), F32),
        in_specs=[VMEM] * 3,
        out_specs=VMEM,
        compiler_params=pltpu.CompilerParams(vmem_limit_bytes=VMEM_END),
        name="lows",
    )(grads, key_b, value_b)


def grad_b_kernel(slots, grads, key_a, value_a, out):
    for kind, down in enumerate((key_a, value_a)):
        low = dot_nt(slots[...], down[...]).astype(BF16)
        out[kind] = dot_tn(low, grads_of(grads, kind))


def run_grad_b(slots, grads, key_a, value_a):
    rank, width = key_a.shape
    return pl.pallas_call(
        grad_b_kernel,
        out_shape=jax.ShapeDtypeStruct((2, rank, grads.shape[-1]), F32),
        in_specs=[VMEM] * 4,
        out_specs=VMEM,
        compiler_params=pltpu.CompilerParams(vmem_limit_bytes=VMEM_END),
        cost_estimate=pl.CostEstimate(
            flops=4 * slots.shape[0] * rank * width, bytes_accessed=1 << 22, transcendentals=0
        ),
        name="grad_b",
    )(slots, grads, key_a, value_a)


def grad_a_kernel(lows, slots, out):
    total = lows[0]
    for k in range(1, MP):
        total = total + lows[k]
    high = total.astype(BF16)
    rest = total - high.astype(F32)
    middle = rest.astype(BF16)
    low = (rest - middle.astype(F32)).astype(BF16)

    def tile(n, carry):
        cols = pl.ds(pl.multiple_of(n * 512, 512), 512)
        some = slots[:, cols]
        out[:, cols] = dot_tn(high, some) + (dot_tn(middle, some) + dot_tn(low, some))
        return carry

    lax.fori_loop(0, slots.shape[1] // 512, tile, 0)


def run_grad_a(lows, slots):
    return pl.pallas_call(
        grad_a_kernel,
        out_shape=jax.ShapeDtypeStruct((lows.shape[2], slots.shape[1]), F32),
        in_specs=[VMEM] * 2,
        out_specs=VMEM,
        compiler_params=pltpu.CompilerParams(vmem_limit_bytes=VMEM_END),
        name="grad_a",
    )(lows, slots)


def local(
    hidden_in,
    slot_hidden,
    norm_gain,
    w_query,
    w_key,
    w_value,
    w_out,
    key_a,
    key_b,
    value_a,
    value_b,
    cotangent,
):
    width = hidden_in.shape[2]
    share = hidden_in.shape[1] // MP
    places = [lax.axis_index(name) for name in ("section", "mp", "dp")]
    info = jnp.stack(places).astype(jnp.int32)
    parts = lax.axis_size("dp")

    like = lambda array: jax.ShapeDtypeStruct(array.shape, BF16)
    block_rows = jax.ShapeDtypeStruct(hidden_in.shape[1:], BF16)
    shapes = {
        "parts": parts,
        "sizes": (*hidden_in.shape[1:], w_query.shape[2]),
        "given": [
            jax.ShapeDtypeStruct(norm_gain.shape, F32),
            block_rows,
            like(w_key),
            like(w_value),
            like(w_query),
            like(w_out),
            jax.ShapeDtypeStruct((MICRO, 2, SLOTS, TILE), BF16),
            jax.ShapeDtypeStruct((parts * MICRO * SLOTS, width), BF16),
        ],
    }
    pieces = []
    kept = []
    for tick in range(TICKS):
        if tick == 0:
            operands = [hidden_in, w_key, w_value, w_query, w_out]
            operands += [slot_hidden[0].reshape(-1, width), key_a[0].T, key_b[0]]
            operands += [value_a[0].T, value_b[0]]
            far = [pltpu.with_memory_space_constraint(x, pltpu.HBM) for x in [norm_gain] + operands]
            found = run_tick(tick, info, far[0], far[1:], shapes, [], [])
            gain, late, wk, wv, wq, wo, slot_kv, slots = found[:8]
            part, *kept = found[8:]
        else:
            operands = [slot_kv, wo] + ([slots, wq, wk, wv] if tick < TICKS - 1 else [])
            if tick < MICRO:
                operands.append(late)
            if SECTIONS - 1 <= tick <= SECTIONS - 1 + MICRO - 1:
                operands.append(cotangent)
            part, *kept = run_tick(tick, info, gain, operands, shapes, pieces, kept)
        if tick + 1 < TICKS:
            arrived = lax.all_to_all(
                part.reshape(MP, share, width),
                ("dp", "section", "mp"),
                0,
                0,
                axis_index_groups=sum_groups(tick, lax.axis_size("dp")),
                tiled=True,
            )
            own_piece = pieces[0] if pieces else None
            send, slots = run_update(
                tick, info, arrived, gain, kept[1], cotangent, own_piece, slots
            )
            sent = {
                offset: lax.ppermute(send, ("section", "mp"), routes(tick, offset))
                for offset in (2, 1, 3, 0)
            }
            pieces = [sent[offset] for offset in range(MP)]
    with jax.named_scope("ends"):
        all_grads = lax.all_to_all(kept[3], "dp", 0, 0, tiled=True)
    up = (key_b[0], value_b[0])
    lows = run_lows(all_grads, *up)
    with jax.named_scope("lows"):
        lows = lax.all_to_all(lows, "mp", 0, 0, tiled=True)
    grad_b = run_grad_b(slots, all_grads, key_a[0].T, value_a[0].T)
    grad_a = run_grad_a(lows, slots).reshape(2, -1, width)
    return (jnp.swapaxes(grad_a, 1, 2)[None], grad_b[None])


def solution(mesh):
    placed = (
        P("dp", None, None),
        P("section", "dp", None, None),
        P("section", None),
        P("section", None, "mp"),
        P("section", None, "mp"),
        P("section", None, "mp"),
        P("section", "mp", None),
        P("section", None, None),
        P("section", None, "mp"),
        P("section", None, None),
        P("section", None, "mp"),
        P("dp", None, None),
    )
    return jax.shard_map(
        local,
        mesh=mesh,
        in_specs=placed,
        out_specs=(P("section", None, None, None), P("section", None, None, "mp")),
        check_vma=False,
    )
```

```python
import functools
import math

import jax
import jax.numpy as jnp
from jax import lax
from jax.experimental import pallas as pl
from jax.experimental.pallas import tpu as pltpu
from jax.sharding import PartitionSpec as P

HD = 128
SLOTS = 16
MICRO = 2
EPS = 1e-05
NEG = -1e30
HIGH = lax.Precision.HIGHEST
SCALE = 1.0 / math.sqrt(HD)
SECTIONS = 4
MP = 4
GROUPS = 2
PER = 3
TILE = 256
TICKS = 2 * SECTIONS + MICRO - 2


F32 = jnp.float32
BF16 = jnp.bfloat16
VMEM = pl.BlockSpec(memory_space=pltpu.VMEM)
HBM = pl.BlockSpec(memory_space=pltpu.HBM)
VMEM_FIRST = 24 << 20
VMEM_TICK = 9 << 20
VMEM_END = 16 << 20
UNROLL_PROJECT = False
UNROLL_GROUPS = True
UNROLL_GRADS = False
VMEM_UPDATE = 4 << 20
SMEM = pl.BlockSpec(memory_space=pltpu.SMEM)


def mixdot(left, right):
    return jnp.dot(left, right, preferred_element_type=F32)


def dot_nt(left, right):
    return lax.dot_general(left, right, (((1,), (1,)), ((), ())), preferred_element_type=F32)


def dot_tn(left, right):
    return lax.dot_general(left, right, (((0,), (0,)), ((), ())), preferred_element_type=F32)


def several(times, step, unroll):
    if unroll:
        for i in range(times):
            step(i)
        return

    def looped(i, carry):
        step(i)
        return carry

    lax.fori_loop(0, times, looped, 0)


def in_flight(index):
    return (index >= 0) & (index < MICRO)


def probabilities(q_three, keys, count):
    scores = dot_nt(q_three, keys) * SCALE
    row = lax.broadcasted_iota(jnp.int32, scores.shape, 0) % count
    col = lax.broadcasted_iota(jnp.int32, scores.shape, 1)
    seen = (col <= row) | ((col >= count) & (col < count + SLOTS))
    scores = jnp.where(seen, scores, NEG)
    top = jnp.max(scores, axis=-1, keepdims=True)
    raised = jnp.exp(scores - top)
    return raised / jnp.sum(raised, axis=-1, keepdims=True)


def slot_rounds(tick):
    table = {0: (2, 3, 4), 1: (0, 3, 4), 2: (0, 1, 6), 3: (0, 1, 2)}
    return [(s, ticks.index(tick)) for s, ticks in table.items() if tick in ticks]


def other_half(place):
    return jnp.where(place < 4, place + 4, place - 4)


def slot_source(place, number):
    return place if number < 2 else other_half(place)


def slot_members(place, number, k):
    if number == 0:
        return 2 * k + place % 2
    return jnp.where(place < 4, 0, 4) + k


def tick_kernel(tick, count, *refs):
    has_pieces = tick > 0
    may_f = tick <= SECTIONS - 2 + MICRO - 1
    may_p = SECTIONS - 1 <= tick <= SECTIONS - 1 + MICRO - 1
    may_b = tick >= SECTIONS - 1
    refs = list(refs)
    take = lambda n: [refs.pop(0) for _ in range(n)]
    info, gain = take(2)
    w_all = hidden = late = None
    if tick == 0:
        hbm = [gain] + take(10)
        gain, late, w_all, wo, slot_kv, slots = take(6)
    elif tick < TICKS - 1:
        slot_kv, wo, slots, w_all = take(4)
    else:
        slot_kv, wo = take(2)
    late = take(1)[0] if 0 < tick < MICRO else late
    cot = take(1)[0] if may_p else None
    pieces = take(MP) if has_pieces else []
    take(kept_before(tick))
    part, kept_qkv, kept_own = take(3)
    kept_slot = take(1)[0] if may_b else None
    ends = take(1)[0] if tick == TICKS - 1 else None
    normed, gbuf, mixed, gtile, *first = refs

    section = info[0]
    me = info[1]
    share = count // MP
    width = part.shape[1]
    b_f = tick - section
    b_b = tick - (2 * SECTIONS - 2) + section
    last = section == SECTIONS - 1
    do_b = in_flight(b_b) if may_b else None

    copies = []
    if tick == 0:
        g_hbm, h_hbm, wk_hbm, wv_hbm, wq_hbm, wo_hbm, *slot_hbm = hbm
        slot_rows, key_a, key_b, value_a, value_b, sems = first
        pairs = [(g_hbm, gain)]
        pairs += list(zip(slot_hbm, (slot_rows, key_a, key_b, value_a, value_b)))
        pairs += [(wk_hbm.at[0], w_all.at[3]), (wv_hbm.at[0], w_all.at[4]), (h_hbm.at[0], gbuf)]
        for j in range(3):
            pairs.append((wq_hbm.at[0, :, pl.ds(j * TILE, TILE)], w_all.at[j]))
        pairs += [(wo_hbm, wo), (h_hbm.at[1], late)]
        copies = [
            pltpu.make_async_copy(source, target, sems.at[i])
            for i, (source, target) in enumerate(pairs)
        ]
        hidden = gbuf
        for copy in copies:
            copy.start()

    def normalize_into(source, place, rows, to=None):
        to = normed if to is None else to

        def some(i, carry):
            part_rows = pl.ds(pl.multiple_of(i * 16, 16), 16)
            wide = source[part_rows].astype(F32)
            inverse = lax.rsqrt(jnp.mean(wide * wide, axis=-1, keepdims=True) + EPS)
            target = pl.ds(pl.multiple_of(place + i * 16, 16), 16)
            to[target] = (wide * inverse * gain[...]).astype(BF16)
            return carry

        lax.fori_loop(0, rows // 16, some, 0)

    def place_of(offset):
        return pl.multiple_of(lax.rem(me + MP - offset, MP) * share, share)

    def gather_pieces():
        for offset in range(MP):
            gbuf[pl.ds(place_of(offset), share)] = pieces[offset][...]

    def project(block):
        normalize_into(gbuf, 0, count)
        kept_own[block] = gbuf[pl.ds(place_of(0), share)]

        def tile(j):
            kept_qkv[block, j] = mixdot(normed[...], w_all[j]).astype(BF16)

        if tick == 0:
            for j in (3, 4, 0, 1, 2):
                if j < 3:
                    copies[9 + j].wait()
                tile(j)
        else:
            several(5, tile, UNROLL_PROJECT)

    def lanes(head):
        if isinstance(head, int):
            return pl.ds(head * HD, HD)
        return pl.ds(pl.multiple_of(head * HD, HD), HD)

    def group_operands(group, block):
        parts = []
        for k in range(PER):
            head = group * PER + k
            parts.append(kept_qkv[block, head // 2, :, lanes(head % 2)])
        q_three = jnp.concatenate(parts, axis=0)
        pad = jnp.zeros((TILE - count - SLOTS, HD), BF16)
        cols = lanes(group)
        keys = jnp.concatenate([kept_qkv[block, 3, :, cols], slot_kv[block, 0, :, cols], pad], axis=0)
        values = jnp.concatenate(
            [kept_qkv[block, 4, :, cols], slot_kv[block, 1, :, cols], pad], axis=0
        )
        return q_three, keys, values

    if tick == 0:
        for copy in copies[:2]:
            copy.wait()
        own_slots = pl.ds(pl.multiple_of(info[2] * MICRO * SLOTS, MICRO * SLOTS), MICRO * SLOTS)
        slot_normed = slots.at[own_slots]
        normalize_into(slot_rows, 0, MICRO * SLOTS, slot_normed)
        for copy in copies[2:9]:
            copy.wait()
        low_key = dot_nt(slot_normed[...], key_a[...]).astype(BF16)
        low_value = dot_nt(slot_normed[...], value_a[...]).astype(BF16)
        slot_keys = mixdot(slot_normed[...], w_all[3]) + mixdot(low_key, key_b[...])
        slot_values = mixdot(slot_normed[...], w_all[4]) + mixdot(low_value, value_b[...])
        for block in range(MICRO):
            rows = slice(block * SLOTS, (block + 1) * SLOTS)
            slot_kv[block, 0] = slot_keys[rows].astype(BF16)
            slot_kv[block, 1] = slot_values[rows].astype(BF16)

        @pl.when(section > 0)
        def _():
            for copy in copies[9:]:
                copy.wait()

    if tick < TICKS - 1:
        for spare, number in slot_rounds(tick):

            @pl.when(section == spare)
            def _():
                source = slot_source(info[2], number)
                for k in range(MP):
                    rows = pl.ds(pl.multiple_of(source * share, share), share)
                    part[k * share : (k + 1) * share] = slots[rows]

    if tick == 1:

        @pl.when(section == 0)
        def _():
            gbuf[...] = late[...]

    if has_pieces:
        moving = in_flight(b_f) & (section > 0)
        if may_b and tick > SECTIONS - 1:
            moving = moving | (do_b & jnp.logical_not(last))

        @pl.when(moving)
        def _():
            gather_pieces()

    if may_f or may_p:

        @pl.when(in_flight(b_f))
        def _():
            project(b_f)

    if may_f:

        @pl.when(in_flight(b_f) & jnp.logical_not(last))
        def _():
            def one_group(group):
                q_three, keys, values = group_operands(group, b_f)
                probs = probabilities(q_three, keys, count)
                heads = mixdot(probs.astype(BF16), values).astype(BF16)
                for k in range(PER):
                    mixed[:, lanes(group * PER + k)] = heads[k * count : (k + 1) * count]

            several(GROUPS, one_group, UNROLL_GROUPS)
            for copy in copies[12:]:
                copy.wait()

            def out_tile(n, carry):
                cols = pl.ds(pl.multiple_of(n * 512, 512), 512)
                part[:, cols] = mixdot(mixed[...], wo[0, :, cols]).astype(BF16)
                return carry

            lax.fori_loop(0, width // 512, out_tile, 0)

    if may_b:
        if may_p:

            @pl.when(do_b & last)
            def _():
                gbuf[...] = cot[b_b]

        @pl.when(do_b)
        def _():
            def grad_tile(j):
                rows = pl.ds(j * TILE if UNROLL_GRADS else pl.multiple_of(j * TILE, TILE), TILE)
                mixed[:, rows] = dot_nt(gbuf[...], wo[0, rows]).astype(BF16)

            several(3, grad_tile, UNROLL_GRADS)

            def one_group(group):
                q_three, keys, values = group_operands(group, b_b)
                probs = probabilities(q_three, keys, count)
                heads = [mixed[:, lanes(group * PER + k)] for k in range(PER)]
                g_three = jnp.concatenate(heads, axis=0)
                grad_probs = dot_nt(g_three, values)
                grad_values = dot_tn(probs.astype(BF16), g_three).astype(BF16)
                centre = jnp.sum(probs * grad_probs, axis=-1, keepdims=True)
                scaled = (probs * (grad_probs - centre) * SCALE).astype(BF16)
                grad_query = mixdot(scaled, keys).astype(BF16)
                grad_keys = dot_tn(scaled, q_three).astype(BF16)
                for k in range(PER):
                    head = group * PER + k
                    gtile[head // 2, :, lanes(head % 2)] = grad_query[k * count : (k + 1) * count]
                cols = lanes(group)
                gtile[3, :, cols] = grad_keys[:count]
                gtile[4, :, cols] = grad_values[:count]
                kept_slot[b_b, 0, :, cols] = grad_keys[count : count + SLOTS]
                kept_slot[b_b, 1, :, cols] = grad_values[count : count + SLOTS]

            several(GROUPS, one_group, UNROLL_GROUPS)

        if tick == TICKS - 1:
            for d in range(ends.shape[0]):
                ends[d] = kept_slot[...]

        if tick < TICKS - 1:

            @pl.when(do_b & (section > 0))
            def _():
                def in_tile(n, carry):
                    cols = pl.ds(pl.multiple_of(n * 512, 512), 512)
                    total = dot_nt(gtile[0], w_all[0, cols])
                    for j in range(1, 5):
                        total = total + dot_nt(gtile[j], w_all[j, cols])
                    part[:, cols] = total.astype(BF16)
                    return carry

                lax.fori_loop(0, width // 512, in_tile, 0)


def kept_before(tick):
    return 0 if tick == 0 else (2 if tick <= SECTIONS - 1 else 3)


def run_tick(tick, info, gain, operands, shapes, pieces, kept):
    count, width, heads = shapes["sizes"]
    share = count // MP
    keep = [
        jax.ShapeDtypeStruct((MICRO, 5, count, TILE), BF16),
        jax.ShapeDtypeStruct((MICRO, share, width), BF16),
    ]
    if tick >= SECTIONS - 1:
        keep.append(jax.ShapeDtypeStruct((MICRO, 2, SLOTS, TILE), BF16))
    ends = []
    if tick == TICKS - 1:
        ends.append(jax.ShapeDtypeStruct((shapes["parts"], *keep[2].shape), BF16))
    operands = operands + list(pieces)
    first_kept = 2 + len(operands)
    given = shapes["given"] if tick == 0 else []
    in_specs = [SMEM] + [VMEM] * (1 + len(operands) + len(kept))
    if tick == 0:
        in_specs[1:] = [HBM] * 11
    scratch = [
        pltpu.VMEM((count, width), BF16),
        pltpu.VMEM((count, width), BF16),
        pltpu.VMEM((count, heads), BF16),
        pltpu.VMEM((5, count, TILE), BF16),
    ]
    if tick == 0:
        scratch += [pltpu.VMEM(array.shape, BF16) for array in operands[5:]]
        scratch.append(pltpu.SemaphoreType.DMA((14,)))
    return pl.pallas_call(
        functools.partial(tick_kernel, tick, count),
        out_shape=given + [jax.ShapeDtypeStruct((count, width), BF16)] + keep + ends,
        in_specs=in_specs,
        out_specs=[VMEM] * (len(given) + 1 + len(keep) + len(ends)),
        scratch_shapes=scratch,
        input_output_aliases={first_kept + i: 1 + i for i in range(len(kept))},
        compiler_params=pltpu.CompilerParams(
            vmem_limit_bytes=VMEM_FIRST if tick == 0 else VMEM_TICK
        ),
        name=f"tick{tick}",
    )(info, gain, *operands, *kept)


def update_kernel(tick, share, *refs):
    may_f = tick <= SECTIONS - 2 + MICRO - 1
    may_b = tick >= SECTIONS - 1
    may_p = SECTIONS - 1 <= tick <= SECTIONS - 1 + MICRO - 1
    refs = list(refs)
    info, arrived, gain, own = refs[:4]
    del refs[:4]
    cot = refs.pop(0) if may_p else None
    piece = refs.pop(0) if may_b else None
    _, out, slots = refs
    section = info[0]
    me = info[1]
    b_f = tick - section
    b_b = tick - (2 * SECTIONS - 2) + section
    last = section == SECTIONS - 1

    for spare, number in slot_rounds(tick):

        @pl.when(section == spare)
        def _():
            for k in range(MP):
                source = slot_source(slot_members(info[2], number, k), number)
                slots[pl.ds(pl.multiple_of(source * share, share), share)] = arrived[k]

    def summed(rows):
        total = arrived[0, rows].astype(F32)
        for k in range(1, MP):
            total = total + arrived[k, rows].astype(F32)
        return total

    def step_back(grad_of):
        def rows_of(i, carry):
            rows = pl.ds(pl.multiple_of(i * 16, 16), 16)
            wide = own[b_b, rows].astype(F32)
            inverse = lax.rsqrt(jnp.mean(wide * wide, axis=-1, keepdims=True) + EPS)
            unit = wide * inverse
            scaled = summed(rows) * gain[...]
            centre = jnp.mean(scaled * unit, axis=-1, keepdims=True)
            change = inverse * (scaled - unit * centre)
            out[rows] = (grad_of(i, rows).astype(F32) + change).astype(BF16)
            return carry

        lax.fori_loop(0, share // 16, rows_of, 0)

    if may_f:

        @pl.when(in_flight(b_f) & jnp.logical_not(last))
        def _():
            def rows_of(i, carry):
                rows = pl.ds(pl.multiple_of(i * 16, 16), 16)
                out[rows] = (own[b_f, rows].astype(F32) + summed(rows)).astype(BF16)
                return carry

            lax.fori_loop(0, share // 16, rows_of, 0)

    if may_p:

        @pl.when(in_flight(b_b) & last)
        def _():
            step_back(lambda i, rows: cot[b_b, pl.ds(pl.multiple_of(me * share + i * 16, 16), 16)])

    if may_b and tick > SECTIONS - 1:

        @pl.when(in_flight(b_b) & (section > 0) & jnp.logical_not(last))
        def _():
            step_back(lambda i, rows: piece[rows])


def run_update(tick, info, arrived, gain, own, cot, piece, slots):
    share, width = arrived.shape[1:]
    operands = [arrived, gain, own]
    if SECTIONS - 1 <= tick <= SECTIONS - 1 + MICRO - 1:
        operands.append(cot)
    if tick >= SECTIONS - 1:
        operands.append(piece)
    operands.append(slots)
    return pl.pallas_call(
        functools.partial(update_kernel, tick, share),
        out_shape=[
            jax.ShapeDtypeStruct((share, width), BF16),
            jax.ShapeDtypeStruct(slots.shape, BF16),
        ],
        in_specs=[SMEM] + [VMEM] * len(operands),
        out_specs=[VMEM] * 2,
        input_output_aliases={len(operands): 1},
        compiler_params=pltpu.CompilerParams(vmem_limit_bytes=VMEM_UPDATE),
        name=f"update{tick}",
    )(info, *operands)


def routes(tick, offset):
    pairs = []
    for section in range(SECTIONS):
        target = None
        if section < SECTIONS - 1 and 0 <= tick - section < MICRO:
            target = section + 1
        if section > 0 and 0 <= tick - (2 * SECTIONS - 2) + section < MICRO:
            target = section - 1
        if target is not None:
            for m in range(MP):
                pairs.append((section * MP + m, target * MP + (m + offset) % MP))
    return pairs


def sum_groups(tick, parts):
    found = []
    for section in range(SECTIONS):
        forward = section < SECTIONS - 1 and 0 <= tick - section < MICRO
        backward = section > 0 and 0 <= tick - (2 * SECTIONS - 2) + section < MICRO
        place = lambda d, m: (d * SECTIONS + section) * MP + m
        if forward or backward:
            found += [[place(d, m) for m in range(MP)] for d in range(parts)]
            continue
        if dict(slot_rounds(tick)).get(section, 0) == 0:
            sets = [[2 * k + low for k in range(MP)] for low in range(2)]
        else:
            sets = [[4 * high + k for k in range(MP)] for high in range(2)]
        found += [[place(d, m) for d in members] for members in sets for m in range(MP)]
    return found


def grads_of(grads, kind):
    blocks = [grads[d, block, kind] for d in range(grads.shape[0]) for block in range(MICRO)]
    return jnp.concatenate(blocks, axis=0)


def lows_kernel(grads, key_b, value_b, out):
    low_key = dot_nt(grads_of(grads, 0), key_b[...])
    low_value = dot_nt(grads_of(grads, 1), value_b[...])
    total = jnp.concatenate([low_key, low_value], axis=1).astype(BF16)
    for k in range(MP):
        out[k] = total


def run_lows(grads, key_b, value_b):
    rows = grads.shape[0] * MICRO * SLOTS
    return pl.pallas_call(
        lows_kernel,
        out_shape=jax.ShapeDtypeStruct((MP, rows, 2 * key_b.shape[0]), BF16),
        in_specs=[VMEM] * 3,
        out_specs=VMEM,
        compiler_params=pltpu.CompilerParams(vmem_limit_bytes=VMEM_END),
        name="lows",
    )(grads, key_b, value_b)


def grad_b_kernel(slots, grads, key_a, value_a, out):
    for kind, down in enumerate((key_a, value_a)):
        low = dot_nt(slots[...], down[...]).astype(BF16)
        out[kind] = dot_tn(low, grads_of(grads, kind))


def run_grad_b(slots, grads, key_a, value_a):
    rank, width = key_a.shape
    return pl.pallas_call(
        grad_b_kernel,
        out_shape=jax.ShapeDtypeStruct((2, rank, grads.shape[-1]), F32),
        in_specs=[VMEM] * 4,
        out_specs=VMEM,
        compiler_params=pltpu.CompilerParams(vmem_limit_bytes=VMEM_END),
        cost_estimate=pl.CostEstimate(
            flops=4 * slots.shape[0] * rank * width, bytes_accessed=1 << 22, transcendentals=0
        ),
        name="grad_b",
    )(slots, grads, key_a, value_a)


def grad_a_kernel(lows, slots, out):
    total = lows[0].astype(F32)
    for k in range(1, MP):
        total = total + lows[k].astype(F32)
    total = total.astype(BF16)

    def tile(n, carry):
        cols = pl.ds(pl.multiple_of(n * 512, 512), 512)
        out[:, cols] = dot_tn(total, slots[:, cols])
        return carry

    lax.fori_loop(0, slots.shape[1] // 512, tile, 0)


def run_grad_a(lows, slots):
    return pl.pallas_call(
        grad_a_kernel,
        out_shape=jax.ShapeDtypeStruct((lows.shape[2], slots.shape[1]), F32),
        in_specs=[VMEM] * 2,
        out_specs=VMEM,
        compiler_params=pltpu.CompilerParams(vmem_limit_bytes=VMEM_END),
        name="grad_a",
    )(lows, slots)


def local(
    hidden_in,
    slot_hidden,
    norm_gain,
    w_query,
    w_key,
    w_value,
    w_out,
    key_a,
    key_b,
    value_a,
    value_b,
    cotangent,
):
    width = hidden_in.shape[2]
    share = hidden_in.shape[1] // MP
    places = [lax.axis_index(name) for name in ("section", "mp", "dp")]
    info = jnp.stack(places).astype(jnp.int32)
    parts = lax.axis_size("dp")

    like = lambda array: jax.ShapeDtypeStruct(array.shape, BF16)
    block_rows = jax.ShapeDtypeStruct(hidden_in.shape[1:], BF16)
    shapes = {
        "parts": parts,
        "sizes": (*hidden_in.shape[1:], w_query.shape[2]),
        "given": [
            jax.ShapeDtypeStruct(norm_gain.shape, F32),
            block_rows,
            jax.ShapeDtypeStruct((5, width, TILE), BF16),
            like(w_out),
            jax.ShapeDtypeStruct((MICRO, 2, SLOTS, TILE), BF16),
            jax.ShapeDtypeStruct((parts * MICRO * SLOTS, width), BF16),
        ],
    }
    pieces = []
    kept = []
    for tick in range(TICKS):
        if tick == 0:
            operands = [hidden_in, w_key, w_value, w_query, w_out]
            operands += [slot_hidden[0].reshape(-1, width), key_a[0].T, key_b[0]]
            operands += [value_a[0].T, value_b[0]]
            far = [pltpu.with_memory_space_constraint(x, pltpu.HBM) for x in [norm_gain] + operands]
            found = run_tick(tick, info, far[0], far[1:], shapes, [], [])
            gain, late, w_all, wo, slot_kv, slots = found[:6]
            part, *kept = found[6:]
        else:
            operands = [slot_kv, wo] + ([slots, w_all] if tick < TICKS - 1 else [])
            if tick < MICRO:
                operands.append(late)
            if SECTIONS - 1 <= tick <= SECTIONS - 1 + MICRO - 1:
                operands.append(cotangent)
            part, *kept = run_tick(tick, info, gain, operands, shapes, pieces, kept)
        if tick + 1 < TICKS:
            arrived = lax.all_to_all(
                part.reshape(MP, share, width),
                ("dp", "section", "mp"),
                0,
                0,
                axis_index_groups=sum_groups(tick, lax.axis_size("dp")),
                tiled=True,
            )
            own_piece = pieces[0] if pieces else None
            send, slots = run_update(
                tick, info, arrived, gain, kept[1], cotangent, own_piece, slots
            )
            sent = {
                offset: lax.ppermute(send, ("section", "mp"), routes(tick, offset))
                for offset in (2, 1, 3, 0)
            }
            pieces = [sent[offset] for offset in range(MP)]
    with jax.named_scope("ends"):
        all_grads = lax.all_to_all(kept[3], "dp", 0, 0, tiled=True)
    up = (key_b[0], value_b[0])
    lows = run_lows(all_grads, *up)
    with jax.named_scope("lows"):
        lows = lax.all_to_all(lows, "mp", 0, 0, tiled=True)
    grad_b = run_grad_b(slots, all_grads, key_a[0].T, value_a[0].T)
    grad_a = run_grad_a(lows, slots).reshape(2, -1, width)
    return (jnp.swapaxes(grad_a, 1, 2)[None], grad_b[None])


def solution(mesh):
    placed = (
        P("dp", None, None),
        P("section", "dp", None, None),
        P("section", None),
        P("section", None, "mp"),
        P("section", None, "mp"),
        P("section", None, "mp"),
        P("section", "mp", None),
        P("section", None, None),
        P("section", None, "mp"),
        P("section", None, None),
        P("section", None, "mp"),
        P("dp", None, None),
    )
    return jax.shard_map(
        local,
        mesh=mesh,
        in_specs=placed,
        out_specs=(P("section", None, None, None), P("section", None, None, "mp")),
        check_vma=False,
    )
```

```python
import functools
import math

import jax
import jax.numpy as jnp
from jax import lax
from jax.experimental import pallas as pl
from jax.experimental.pallas import tpu as pltpu
from jax.sharding import PartitionSpec as P

HD = 128
SLOTS = 16
MICRO = 2
EPS = 1e-05
NEG = -1e30
HIGH = lax.Precision.HIGHEST
SCALE = 1.0 / math.sqrt(HD)
SECTIONS = 4
MP = 4
GROUPS = 2
PER = 3
TILE = 256
TICKS = 2 * SECTIONS + MICRO - 2


F32 = jnp.float32
BF16 = jnp.bfloat16
VMEM = pl.BlockSpec(memory_space=pltpu.VMEM)
HBM = pl.BlockSpec(memory_space=pltpu.HBM)
VMEM_FIRST = 24 << 20
VMEM_TICK = 9 << 20
VMEM_END = 16 << 20
UNROLL_PROJECT = 3
UNROLL_GROUPS = True
UNROLL_GRADS = False
VMEM_UPDATE = 4 << 20
SMEM = pl.BlockSpec(memory_space=pltpu.SMEM)


def mixdot(left, right):
    return jnp.dot(left, right, preferred_element_type=F32)


def dot_nt(left, right):
    return lax.dot_general(left, right, (((1,), (1,)), ((), ())), preferred_element_type=F32)


def dot_tn(left, right):
    return lax.dot_general(left, right, (((0,), (0,)), ((), ())), preferred_element_type=F32)


def several(times, step, unroll):
    if unroll:
        for i in range(times):
            step(i)
        return

    def looped(i, carry):
        step(i)
        return carry

    lax.fori_loop(0, times, looped, 0)


def in_flight(index):
    return (index >= 0) & (index < MICRO)


def probabilities(q_three, keys, count):
    scores = dot_nt(q_three, keys) * SCALE
    row = lax.broadcasted_iota(jnp.int32, scores.shape, 0) % count
    col = lax.broadcasted_iota(jnp.int32, scores.shape, 1)
    seen = (col <= row) | ((col >= count) & (col < count + SLOTS))
    scores = jnp.where(seen, scores, NEG)
    top = jnp.max(scores, axis=-1, keepdims=True)
    raised = jnp.exp(scores - top)
    return raised / jnp.sum(raised, axis=-1, keepdims=True)


def slot_rounds(tick):
    table = {0: (2, 3, 4), 1: (0, 3, 4), 2: (0, 1, 6), 3: (0, 1, 2)}
    return [(s, ticks.index(tick)) for s, ticks in table.items() if tick in ticks]


def other_half(place):
    return jnp.where(place < 4, place + 4, place - 4)


def slot_source(place, number):
    return place if number < 2 else other_half(place)


def slot_members(place, number, k):
    if number == 0:
        return 2 * k + place % 2
    return jnp.where(place < 4, 0, 4) + k


def tick_kernel(tick, count, *refs):
    has_pieces = tick > 0
    may_f = tick <= SECTIONS - 2 + MICRO - 1
    may_p = SECTIONS - 1 <= tick <= SECTIONS - 1 + MICRO - 1
    may_b = tick >= SECTIONS - 1
    refs = list(refs)
    take = lambda n: [refs.pop(0) for _ in range(n)]
    info, gain = take(2)
    w_all = hidden = late = None
    if tick == 0:
        hbm = [gain] + take(10)
        gain, late, w_all, wo, slot_kv, slots = take(6)
    elif tick < TICKS - 1:
        slot_kv, wo, slots, w_all = take(4)
    else:
        slot_kv, wo = take(2)
    late = take(1)[0] if 0 < tick < MICRO else late
    cot = take(1)[0] if may_p else None
    pieces = take(MP) if has_pieces else []
    take(kept_before(tick))
    part, kept_qkv, kept_own = take(3)
    kept_slot = take(1)[0] if may_b else None
    ends = take(1)[0] if tick == TICKS - 1 else None
    normed, gbuf, mixed, gtile, *first = refs

    section = info[0]
    me = info[1]
    share = count // MP
    width = part.shape[1]
    b_f = tick - section
    b_b = tick - (2 * SECTIONS - 2) + section
    last = section == SECTIONS - 1
    do_b = in_flight(b_b) if may_b else None

    def columns(j):
        return pl.ds(j * TILE if isinstance(j, int) else pl.multiple_of(j * TILE, TILE), TILE)

    copies = []
    if tick == 0:
        g_hbm, h_hbm, wk_hbm, wv_hbm, wq_hbm, wo_hbm, *slot_hbm = hbm
        slot_rows, key_a, key_b, value_a, value_b, sems = first
        pairs = [(g_hbm, gain)]
        pairs += list(zip(slot_hbm, (slot_rows, key_a, key_b, value_a, value_b)))
        pairs += [(wk_hbm.at[0], w_all.at[:, columns(3)]), (wv_hbm.at[0], w_all.at[:, columns(4)])]
        pairs += [(h_hbm.at[0], gbuf)]
        for j in range(3):
            pairs.append((wq_hbm.at[0, :, columns(j)], w_all.at[:, columns(j)]))
        pairs += [(wo_hbm, wo), (h_hbm.at[1], late)]
        copies = [
            pltpu.make_async_copy(source, target, sems.at[i])
            for i, (source, target) in enumerate(pairs)
        ]
        hidden = gbuf
        for copy in copies:
            copy.start()

    def normalize_into(source, place, rows, to=None):
        to = normed if to is None else to

        def some(i, carry):
            part_rows = pl.ds(pl.multiple_of(i * 16, 16), 16)
            wide = source[part_rows].astype(F32)
            inverse = lax.rsqrt(jnp.mean(wide * wide, axis=-1, keepdims=True) + EPS)
            target = pl.ds(pl.multiple_of(place + i * 16, 16), 16)
            to[target] = (wide * inverse * gain[...]).astype(BF16)
            return carry

        lax.fori_loop(0, rows // 16, some, 0)

    def place_of(offset):
        return pl.multiple_of(lax.rem(me + MP - offset, MP) * share, share)

    def gather_pieces():
        for offset in range(MP):
            gbuf[pl.ds(place_of(offset), share)] = pieces[offset][...]

    def project(block):
        normalize_into(gbuf, 0, count)
        kept_own[block] = gbuf[pl.ds(place_of(0), share)]

        def tile(j):
            kept_qkv[block, j] = mixdot(normed[...], w_all[:, columns(j)]).astype(BF16)

        if tick == 0:
            for j in (3, 4, 0, 1, 2):
                if j < 3:
                    copies[9 + j].wait()
                tile(j)
        else:
            several(5, tile, tick < UNROLL_PROJECT)

    def lanes(head):
        if isinstance(head, int):
            return pl.ds(head * HD, HD)
        return pl.ds(pl.multiple_of(head * HD, HD), HD)

    def group_operands(group, block):
        parts = []
        for k in range(PER):
            head = group * PER + k
            parts.append(kept_qkv[block, head // 2, :, lanes(head % 2)])
        q_three = jnp.concatenate(parts, axis=0)
        pad = jnp.zeros((TILE - count - SLOTS, HD), BF16)
        cols = lanes(group)
        keys = jnp.concatenate([kept_qkv[block, 3, :, cols], slot_kv[block, 0, :, cols], pad], axis=0)
        values = jnp.concatenate(
            [kept_qkv[block, 4, :, cols], slot_kv[block, 1, :, cols], pad], axis=0
        )
        return q_three, keys, values

    if tick == 0:
        for copy in copies[:2]:
            copy.wait()
        own_slots = pl.ds(pl.multiple_of(info[2] * MICRO * SLOTS, MICRO * SLOTS), MICRO * SLOTS)
        slot_normed = slots.at[own_slots]
        normalize_into(slot_rows, 0, MICRO * SLOTS, slot_normed)
        for copy in copies[2:9]:
            copy.wait()
        low_key = dot_nt(slot_normed[...], key_a[...]).astype(BF16)
        low_value = dot_nt(slot_normed[...], value_a[...]).astype(BF16)
        slot_keys = mixdot(slot_normed[...], w_all[:, columns(3)]) + mixdot(low_key, key_b[...])
        slot_values = mixdot(slot_normed[...], w_all[:, columns(4)]) + mixdot(low_value, value_b[...])
        for block in range(MICRO):
            rows = slice(block * SLOTS, (block + 1) * SLOTS)
            slot_kv[block, 0] = slot_keys[rows].astype(BF16)
            slot_kv[block, 1] = slot_values[rows].astype(BF16)

        @pl.when(section > 0)
        def _():
            for copy in copies[9:]:
                copy.wait()

    if tick < TICKS - 1:
        for spare, number in slot_rounds(tick):

            @pl.when(section == spare)
            def _():
                source = slot_source(info[2], number)
                rows = pl.ds(pl.multiple_of(source * share, share), share)

                def fill(k):
                    part[pl.ds(pl.multiple_of(k * share, share), share)] = slots[rows]

                several(MP, fill, False)

    if tick == 1:

        @pl.when(section == 0)
        def _():
            gbuf[...] = late[...]

    if has_pieces:
        moving = in_flight(b_f) & (section > 0)
        if may_b and tick > SECTIONS - 1:
            moving = moving | (do_b & jnp.logical_not(last))

        @pl.when(moving)
        def _():
            gather_pieces()

    if may_f or may_p:

        @pl.when(in_flight(b_f))
        def _():
            project(b_f)

    if may_f:

        @pl.when(in_flight(b_f) & jnp.logical_not(last))
        def _():
            def one_group(group):
                q_three, keys, values = group_operands(group, b_f)
                probs = probabilities(q_three, keys, count)
                heads = mixdot(probs.astype(BF16), values).astype(BF16)
                for k in range(PER):
                    mixed[:, lanes(group * PER + k)] = heads[k * count : (k + 1) * count]

            several(GROUPS, one_group, UNROLL_GROUPS)
            for copy in copies[12:]:
                copy.wait()

            def out_tile(n, carry):
                cols = pl.ds(pl.multiple_of(n * 512, 512), 512)
                part[:, cols] = mixdot(mixed[...], wo[0, :, cols]).astype(BF16)
                return carry

            lax.fori_loop(0, width // 512, out_tile, 0)

    if may_b:
        if may_p:

            @pl.when(do_b & last)
            def _():
                gbuf[...] = cot[b_b]

        @pl.when(do_b)
        def _():
            def grad_tile(j):
                rows = pl.ds(j * TILE if UNROLL_GRADS else pl.multiple_of(j * TILE, TILE), TILE)
                mixed[:, rows] = dot_nt(gbuf[...], wo[0, rows]).astype(BF16)

            several(3, grad_tile, UNROLL_GRADS)

            def one_group(group):
                q_three, keys, values = group_operands(group, b_b)
                probs = probabilities(q_three, keys, count)
                heads = [mixed[:, lanes(group * PER + k)] for k in range(PER)]
                g_three = jnp.concatenate(heads, axis=0)
                grad_probs = dot_nt(g_three, values)
                grad_values = dot_tn(probs.astype(BF16), g_three).astype(BF16)
                centre = jnp.sum(probs * grad_probs, axis=-1, keepdims=True)
                scaled = (probs * (grad_probs - centre) * SCALE).astype(BF16)
                grad_query = mixdot(scaled, keys).astype(BF16)
                grad_keys = dot_tn(scaled, q_three).astype(BF16)
                for k in range(PER):
                    head = group * PER + k
                    gtile[:, lanes(head)] = grad_query[k * count : (k + 1) * count]
                cols = lanes(group)
                gtile[:, lanes(GROUPS * PER + group)] = grad_keys[:count]
                gtile[:, lanes(GROUPS * PER + GROUPS + group)] = grad_values[:count]
                kept_slot[b_b, 0, :, cols] = grad_keys[count : count + SLOTS]
                kept_slot[b_b, 1, :, cols] = grad_values[count : count + SLOTS]

            several(GROUPS, one_group, UNROLL_GROUPS)

        if tick == TICKS - 1:
            for d in range(ends.shape[0]):
                ends[d] = kept_slot[...]

        if tick < TICKS - 1:

            @pl.when(do_b & (section > 0))
            def _():
                def in_tile(n, carry):
                    cols = pl.ds(pl.multiple_of(n * 512, 512), 512)
                    part[:, cols] = dot_nt(gtile[...], w_all[cols]).astype(BF16)
                    return carry

                lax.fori_loop(0, width // 512, in_tile, 0)


def kept_before(tick):
    return 0 if tick == 0 else (2 if tick <= SECTIONS - 1 else 3)


def run_tick(tick, info, gain, operands, shapes, pieces, kept):
    count, width, heads = shapes["sizes"]
    share = count // MP
    keep = [
        jax.ShapeDtypeStruct((MICRO, 5, count, TILE), BF16),
        jax.ShapeDtypeStruct((MICRO, share, width), BF16),
    ]
    if tick >= SECTIONS - 1:
        keep.append(jax.ShapeDtypeStruct((MICRO, 2, SLOTS, TILE), BF16))
    ends = []
    if tick == TICKS - 1:
        ends.append(jax.ShapeDtypeStruct((shapes["parts"], *keep[2].shape), BF16))
    operands = operands + list(pieces)
    first_kept = 2 + len(operands)
    given = shapes["given"] if tick == 0 else []
    in_specs = [SMEM] + [VMEM] * (1 + len(operands) + len(kept))
    if tick == 0:
        in_specs[1:] = [HBM] * 11
    scratch = [
        pltpu.VMEM((count, width), BF16),
        pltpu.VMEM((count, width), BF16),
        pltpu.VMEM((count, heads), BF16),
        pltpu.VMEM((count, 5 * TILE), BF16),
    ]
    if tick == 0:
        scratch += [pltpu.VMEM(array.shape, BF16) for array in operands[5:]]
        scratch.append(pltpu.SemaphoreType.DMA((14,)))
    return pl.pallas_call(
        functools.partial(tick_kernel, tick, count),
        out_shape=given + [jax.ShapeDtypeStruct((count, width), BF16)] + keep + ends,
        in_specs=in_specs,
        out_specs=[VMEM] * (len(given) + 1 + len(keep) + len(ends)),
        scratch_shapes=scratch,
        input_output_aliases={first_kept + i: 1 + i for i in range(len(kept))},
        compiler_params=pltpu.CompilerParams(
            vmem_limit_bytes=VMEM_FIRST if tick == 0 else VMEM_TICK
        ),
        name=f"tick{tick}",
    )(info, gain, *operands, *kept)


def update_kernel(tick, share, *refs):
    may_f = tick <= SECTIONS - 2 + MICRO - 1
    may_b = tick >= SECTIONS - 1
    may_p = SECTIONS - 1 <= tick <= SECTIONS - 1 + MICRO - 1
    refs = list(refs)
    info, arrived, gain, own = refs[:4]
    del refs[:4]
    cot = refs.pop(0) if may_p else None
    piece = refs.pop(0) if tick >= SECTIONS else None
    _, out, slots = refs
    section = info[0]
    me = info[1]
    b_f = tick - section
    b_b = tick - (2 * SECTIONS - 2) + section
    last = section == SECTIONS - 1

    for spare, number in slot_rounds(tick):

        @pl.when(section == spare)
        def _():
            def take(k):
                source = slot_source(slot_members(info[2], number, k), number)
                slots[pl.ds(pl.multiple_of(source * share, share), share)] = arrived[k]

            several(MP, take, False)

    def summed(rows):
        total = arrived[0, rows].astype(F32)
        for k in range(1, MP):
            total = total + arrived[k, rows].astype(F32)
        return total

    def step_back(grad_of):
        def rows_of(i, carry):
            rows = pl.ds(pl.multiple_of(i * 16, 16), 16)
            wide = own[b_b, rows].astype(F32)
            inverse = lax.rsqrt(jnp.mean(wide * wide, axis=-1, keepdims=True) + EPS)
            unit = wide * inverse
            scaled = summed(rows) * gain[...]
            centre = jnp.mean(scaled * unit, axis=-1, keepdims=True)
            change = inverse * (scaled - unit * centre)
            out[rows] = (grad_of(i, rows).astype(F32) + change).astype(BF16)
            return carry

        lax.fori_loop(0, share // 16, rows_of, 0)

    if may_f:

        @pl.when(in_flight(b_f) & jnp.logical_not(last))
        def _():
            def rows_of(i, carry):
                rows = pl.ds(pl.multiple_of(i * 16, 16), 16)
                out[rows] = (own[b_f, rows].astype(F32) + summed(rows)).astype(BF16)
                return carry

            lax.fori_loop(0, share // 16, rows_of, 0)

    if may_b:

        @pl.when(in_flight(b_b) & (section > 0))
        def _():
            def grad_of(i, rows):
                if not may_p:
                    return piece[rows]
                given = cot[b_b, pl.ds(pl.multiple_of(me * share + i * 16, 16), 16)]
                if tick == SECTIONS - 1:
                    return given
                return jnp.where(last, given.astype(F32), piece[rows].astype(F32))

            step_back(grad_of)


def run_update(tick, info, arrived, gain, own, cot, piece, slots):
    share, width = arrived.shape[1:]
    operands = [arrived, gain, own]
    if SECTIONS - 1 <= tick <= SECTIONS - 1 + MICRO - 1:
        operands.append(cot)
    if tick >= SECTIONS:
        operands.append(piece)
    operands.append(slots)
    return pl.pallas_call(
        functools.partial(update_kernel, tick, share),
        out_shape=[
            jax.ShapeDtypeStruct((share, width), BF16),
            jax.ShapeDtypeStruct(slots.shape, BF16),
        ],
        in_specs=[SMEM] + [VMEM] * len(operands),
        out_specs=[VMEM] * 2,
        input_output_aliases={len(operands): 1},
        compiler_params=pltpu.CompilerParams(vmem_limit_bytes=VMEM_UPDATE),
        name=f"update{tick}",
    )(info, *operands)


def routes(tick, offset):
    pairs = []
    for section in range(SECTIONS):
        target = None
        if section < SECTIONS - 1 and 0 <= tick - section < MICRO:
            target = section + 1
        if section > 0 and 0 <= tick - (2 * SECTIONS - 2) + section < MICRO:
            target = section - 1
        if target is not None:
            for m in range(MP):
                pairs.append((section * MP + m, target * MP + (m + offset) % MP))
    return pairs


def sum_groups(tick, parts):
    found = []
    for section in range(SECTIONS):
        forward = section < SECTIONS - 1 and 0 <= tick - section < MICRO
        backward = section > 0 and 0 <= tick - (2 * SECTIONS - 2) + section < MICRO
        place = lambda d, m: (d * SECTIONS + section) * MP + m
        if forward or backward:
            found += [[place(d, m) for m in range(MP)] for d in range(parts)]
            continue
        if dict(slot_rounds(tick)).get(section, 0) == 0:
            sets = [[2 * k + low for k in range(MP)] for low in range(2)]
        else:
            sets = [[4 * high + k for k in range(MP)] for high in range(2)]
        found += [[place(d, m) for d in members] for members in sets for m in range(MP)]
    return found


def grads_of(grads, kind):
    blocks = [grads[d, block, kind] for d in range(grads.shape[0]) for block in range(MICRO)]
    return jnp.concatenate(blocks, axis=0)


def lows_kernel(grads, key_b, value_b, out):
    low_key = dot_nt(grads_of(grads, 0), key_b[...])
    low_value = dot_nt(grads_of(grads, 1), value_b[...])
    total = jnp.concatenate([low_key, low_value], axis=1).astype(BF16)
    for k in range(MP):
        out[k] = total


def run_lows(grads, key_b, value_b):
    rows = grads.shape[0] * MICRO * SLOTS
    return pl.pallas_call(
        lows_kernel,
        out_shape=jax.ShapeDtypeStruct((MP, rows, 2 * key_b.shape[0]), BF16),
        in_specs=[VMEM] * 3,
        out_specs=VMEM,
        compiler_params=pltpu.CompilerParams(vmem_limit_bytes=VMEM_END),
        name="lows",
    )(grads, key_b, value_b)


def grad_b_kernel(slots, grads, key_a, value_a, out):
    for kind, down in enumerate((key_a, value_a)):
        low = dot_nt(slots[...], down[...]).astype(BF16)
        out[kind] = dot_tn(low, grads_of(grads, kind))


def run_grad_b(slots, grads, key_a, value_a):
    rank, width = key_a.shape
    return pl.pallas_call(
        grad_b_kernel,
        out_shape=jax.ShapeDtypeStruct((2, rank, grads.shape[-1]), F32),
        in_specs=[VMEM] * 4,
        out_specs=VMEM,
        compiler_params=pltpu.CompilerParams(vmem_limit_bytes=VMEM_END),
        cost_estimate=pl.CostEstimate(
            flops=4 * slots.shape[0] * rank * width, bytes_accessed=1 << 22, transcendentals=0
        ),
        name="grad_b",
    )(slots, grads, key_a, value_a)


def grad_a_kernel(lows, slots, out):
    total = lows[0].astype(F32)
    for k in range(1, MP):
        total = total + lows[k].astype(F32)
    total = total.astype(BF16)

    out[...] = mixdot(total.T, slots[...])


def run_grad_a(lows, slots):
    return pl.pallas_call(
        grad_a_kernel,
        out_shape=jax.ShapeDtypeStruct((lows.shape[2], slots.shape[1]), F32),
        grid=(4,),
        in_specs=[
            pl.BlockSpec(lows.shape, lambda n: (0, 0, 0)),
            pl.BlockSpec((slots.shape[0], slots.shape[1] // 4), lambda n: (0, n)),
        ],
        out_specs=pl.BlockSpec((lows.shape[2], slots.shape[1] // 4), lambda n: (0, n)),
        compiler_params=pltpu.CompilerParams(vmem_limit_bytes=VMEM_END),
        name="grad_a",
    )(lows, slots)


def local(
    hidden_in,
    slot_hidden,
    norm_gain,
    w_query,
    w_key,
    w_value,
    w_out,
    key_a,
    key_b,
    value_a,
    value_b,
    cotangent,
):
    width = hidden_in.shape[2]
    share = hidden_in.shape[1] // MP
    places = [lax.axis_index(name) for name in ("section", "mp", "dp")]
    info = jnp.stack(places).astype(jnp.int32)
    parts = lax.axis_size("dp")

    like = lambda array: jax.ShapeDtypeStruct(array.shape, BF16)
    block_rows = jax.ShapeDtypeStruct(hidden_in.shape[1:], BF16)
    shapes = {
        "parts": parts,
        "sizes": (*hidden_in.shape[1:], w_query.shape[2]),
        "given": [
            jax.ShapeDtypeStruct(norm_gain.shape, F32),
            block_rows,
            jax.ShapeDtypeStruct((width, 5 * TILE), BF16),
            like(w_out),
            jax.ShapeDtypeStruct((MICRO, 2, SLOTS, TILE), BF16),
            jax.ShapeDtypeStruct((parts * MICRO * SLOTS, width), BF16),
        ],
    }
    pieces = []
    kept = []
    for tick in range(TICKS):
        if tick == 0:
            operands = [hidden_in, w_key, w_value, w_query, w_out]
            operands += [slot_hidden[0].reshape(-1, width), key_a[0].T, key_b[0]]
            operands += [value_a[0].T, value_b[0]]
            far = [pltpu.with_memory_space_constraint(x, pltpu.HBM) for x in [norm_gain] + operands]
            found = run_tick(tick, info, far[0], far[1:], shapes, [], [])
            gain, late, w_all, wo, slot_kv, slots = found[:6]
            part, *kept = found[6:]
        else:
            operands = [slot_kv, wo] + ([slots, w_all] if tick < TICKS - 1 else [])
            if tick < MICRO:
                operands.append(late)
            if SECTIONS - 1 <= tick <= SECTIONS - 1 + MICRO - 1:
                operands.append(cotangent)
            part, *kept = run_tick(tick, info, gain, operands, shapes, pieces, kept)
        if tick + 1 < TICKS:
            arrived = lax.all_to_all(
                part.reshape(MP, share, width),
                ("dp", "section", "mp"),
                0,
                0,
                axis_index_groups=sum_groups(tick, lax.axis_size("dp")),
                tiled=True,
            )
            own_piece = pieces[0] if pieces else None
            send, slots = run_update(
                tick, info, arrived, gain, kept[1], cotangent, own_piece, slots
            )
            sent = {
                offset: lax.ppermute(send, ("section", "mp"), routes(tick, offset))
                for offset in (2, 1, 3, 0)
            }
            pieces = [sent[offset] for offset in range(MP)]
    with jax.named_scope("ends"):
        all_grads = lax.all_to_all(kept[3], "dp", 0, 0, tiled=True)
    up = (key_b[0], value_b[0])
    lows = run_lows(all_grads, *up)
    with jax.named_scope("lows"):
        lows = lax.all_to_all(lows, "mp", 0, 0, tiled=True)
    grad_b = run_grad_b(slots, all_grads, key_a[0].T, value_a[0].T)
    grad_a = run_grad_a(lows, slots).reshape(2, -1, width)
    return (jnp.swapaxes(grad_a, 1, 2)[None], grad_b[None])


def solution(mesh):
    placed = (
        P("dp", None, None),
        P("section", "dp", None, None),
        P("section", None),
        P("section", None, "mp"),
        P("section", None, "mp"),
        P("section", None, "mp"),
        P("section", "mp", None),
        P("section", None, None),
        P("section", None, "mp"),
        P("section", None, None),
        P("section", None, "mp"),
        P("dp", None, None),
    )
    return jax.shard_map(
        local,
        mesh=mesh,
        in_specs=placed,
        out_specs=(P("section", None, None, None), P("section", None, None, "mp")),
        check_vma=False,
    )
```

```python
import functools
import math

import jax
import jax.numpy as jnp
from jax import lax
from jax.experimental import pallas as pl
from jax.experimental.pallas import tpu as pltpu
from jax.sharding import PartitionSpec as P

HD = 128
SLOTS = 16
MICRO = 2
EPS = 1e-05
NEG = -1e30
HIGH = lax.Precision.HIGHEST
SCALE = 1.0 / math.sqrt(HD)
SECTIONS = 4
MP = 4
GROUPS = 2
PER = 3
TILE = 256
TICKS = 2 * SECTIONS + MICRO - 2


F32 = jnp.float32
BF16 = jnp.bfloat16
VMEM = pl.BlockSpec(memory_space=pltpu.VMEM)
HBM = pl.BlockSpec(memory_space=pltpu.HBM)
VMEM_FIRST = 24 << 20
VMEM_TICK = 9 << 20
VMEM_END = 16 << 20
UNROLL_PROJECT = 3
UNROLL_GROUPS = True
UNROLL_GRADS = TICKS - 1
VMEM_UPDATE = 4 << 20
SMEM = pl.BlockSpec(memory_space=pltpu.SMEM)


def mixdot(left, right):
    return jnp.dot(left, right, preferred_element_type=F32)


def dot_nt(left, right):
    return lax.dot_general(left, right, (((1,), (1,)), ((), ())), preferred_element_type=F32)


def dot_tn(left, right):
    return lax.dot_general(left, right, (((0,), (0,)), ((), ())), preferred_element_type=F32)


def several(times, step, unroll):
    if unroll:
        for i in range(times):
            step(i)
        return

    def looped(i, carry):
        step(i)
        return carry

    lax.fori_loop(0, times, looped, 0)


def in_flight(index):
    return (index >= 0) & (index < MICRO)


def probabilities(q_three, keys, count):
    scores = dot_nt(q_three, keys) * SCALE
    row = lax.broadcasted_iota(jnp.int32, scores.shape, 0) % count
    col = lax.broadcasted_iota(jnp.int32, scores.shape, 1)
    seen = (col <= row) | ((col >= count) & (col < count + SLOTS))
    scores = jnp.where(seen, scores, NEG)
    top = jnp.max(scores, axis=-1, keepdims=True)
    raised = jnp.exp(scores - top)
    return raised / jnp.sum(raised, axis=-1, keepdims=True)


def slot_rounds(tick):
    table = {0: (2, 3, 4), 1: (0, 3, 4), 2: (0, 1, 6), 3: (0, 1, 2)}
    return [(s, ticks.index(tick)) for s, ticks in table.items() if tick in ticks]


def other_half(place):
    return jnp.where(place < 4, place + 4, place - 4)


def slot_source(place, number):
    return place if number < 2 else other_half(place)


def slot_members(place, number, k):
    if number == 0:
        return 2 * k + place % 2
    return jnp.where(place < 4, 0, 4) + k


def tick_kernel(tick, count, *refs):
    has_pieces = tick > 0
    may_f = tick <= SECTIONS - 2 + MICRO - 1
    may_p = SECTIONS - 1 <= tick <= SECTIONS - 1 + MICRO - 1
    may_b = tick >= SECTIONS - 1
    refs = list(refs)
    take = lambda n: [refs.pop(0) for _ in range(n)]
    info, gain = take(2)
    w_all = hidden = late = None
    if tick == 0:
        hbm = [gain] + take(10)
        gain, late, w_all, wo, slot_kv, slots = take(6)
    elif tick < TICKS - 1:
        slot_kv, wo, slots, w_all = take(4)
    else:
        slot_kv, wo = take(2)
    late = take(1)[0] if 0 < tick < MICRO else late
    cot = take(1)[0] if may_p else None
    pieces = take(MP) if has_pieces else []
    take(kept_before(tick))
    part, kept_qkv, kept_own = take(3)
    kept_slot = take(1)[0] if may_b else None
    ends = take(1)[0] if tick == TICKS - 1 else None
    normed, gbuf, mixed, gtile, *first = refs

    section = info[0]
    me = info[1]
    share = count // MP
    width = part.shape[1]
    b_f = tick - section
    b_b = tick - (2 * SECTIONS - 2) + section
    last = section == SECTIONS - 1
    do_b = in_flight(b_b) if may_b else None

    def columns(j):
        return pl.ds(j * TILE if isinstance(j, int) else pl.multiple_of(j * TILE, TILE), TILE)

    copies = []
    if tick == 0:
        g_hbm, h_hbm, wk_hbm, wv_hbm, wq_hbm, wo_hbm, *slot_hbm = hbm
        slot_rows, key_a, key_b, value_a, value_b, sems = first
        pairs = [(g_hbm, gain)]
        pairs += list(zip(slot_hbm, (slot_rows, key_a, key_b, value_a, value_b)))
        pairs += [(wk_hbm.at[0], w_all.at[:, columns(3)]), (wv_hbm.at[0], w_all.at[:, columns(4)])]
        pairs += [(h_hbm.at[0], gbuf)]
        for j in range(3):
            pairs.append((wq_hbm.at[0, :, columns(j)], w_all.at[:, columns(j)]))
        pairs += [(wo_hbm, wo), (h_hbm.at[1], late)]
        copies = [
            pltpu.make_async_copy(source, target, sems.at[i])
            for i, (source, target) in enumerate(pairs)
        ]
        hidden = gbuf
        for copy in copies:
            copy.start()

    def normalize_into(source, place, rows, to=None):
        to = normed if to is None else to

        def some(i, carry):
            part_rows = pl.ds(pl.multiple_of(i * 16, 16), 16)
            wide = source[part_rows].astype(F32)
            inverse = lax.rsqrt(jnp.mean(wide * wide, axis=-1, keepdims=True) + EPS)
            target = pl.ds(pl.multiple_of(place + i * 16, 16), 16)
            to[target] = (wide * inverse * gain[...]).astype(BF16)
            return carry

        lax.fori_loop(0, rows // 16, some, 0)

    def place_of(offset):
        return pl.multiple_of(lax.rem(me + MP - offset, MP) * share, share)

    def gather_pieces():
        for offset in range(MP):
            gbuf[pl.ds(place_of(offset), share)] = pieces[offset][...]

    def project(block):
        normalize_into(gbuf, 0, count)
        kept_own[block] = gbuf[pl.ds(place_of(0), share)]

        def tile(j):
            kept_qkv[block, j] = mixdot(normed[...], w_all[:, columns(j)]).astype(BF16)

        if tick == 0:
            for j in (3, 4, 0, 1, 2):
                if j < 3:
                    copies[9 + j].wait()
                tile(j)
        else:
            several(5, tile, tick < UNROLL_PROJECT)

    def lanes(head):
        if isinstance(head, int):
            return pl.ds(head * HD, HD)
        return pl.ds(pl.multiple_of(head * HD, HD), HD)

    def group_operands(group, block):
        parts = []
        for k in range(PER):
            head = group * PER + k
            parts.append(kept_qkv[block, head // 2, :, lanes(head % 2)])
        q_three = jnp.concatenate(parts, axis=0)
        pad = jnp.zeros((TILE - count - SLOTS, HD), BF16)
        cols = lanes(group)
        keys = jnp.concatenate([kept_qkv[block, 3, :, cols], slot_kv[block, 0, :, cols], pad], axis=0)
        values = jnp.concatenate(
            [kept_qkv[block, 4, :, cols], slot_kv[block, 1, :, cols], pad], axis=0
        )
        return q_three, keys, values

    if tick == 0:
        for copy in copies[:2]:
            copy.wait()
        own_slots = pl.ds(pl.multiple_of(info[2] * MICRO * SLOTS, MICRO * SLOTS), MICRO * SLOTS)
        slot_normed = slots.at[own_slots]
        normalize_into(slot_rows, 0, MICRO * SLOTS, slot_normed)
        for copy in copies[2:9]:
            copy.wait()
        low_key = dot_nt(slot_normed[...], key_a[...]).astype(BF16)
        low_value = dot_nt(slot_normed[...], value_a[...]).astype(BF16)
        slot_keys = mixdot(slot_normed[...], w_all[:, columns(3)]) + mixdot(low_key, key_b[...])
        slot_values = mixdot(slot_normed[...], w_all[:, columns(4)]) + mixdot(low_value, value_b[...])
        for block in range(MICRO):
            rows = slice(block * SLOTS, (block + 1) * SLOTS)
            slot_kv[block, 0] = slot_keys[rows].astype(BF16)
            slot_kv[block, 1] = slot_values[rows].astype(BF16)

        @pl.when(section > 0)
        def _():
            for copy in copies[9:]:
                copy.wait()

    if tick < TICKS - 1:
        for spare, number in slot_rounds(tick):

            @pl.when(section == spare)
            def _():
                source = slot_source(info[2], number)
                rows = pl.ds(pl.multiple_of(source * share, share), share)

                def fill(k):
                    part[pl.ds(pl.multiple_of(k * share, share), share)] = slots[rows]

                several(MP, fill, False)

    if tick == 1:

        @pl.when(section == 0)
        def _():
            gbuf[...] = late[...]

    if has_pieces:
        moving = in_flight(b_f) & (section > 0)
        if may_b and tick > SECTIONS - 1:
            moving = moving | (do_b & jnp.logical_not(last))

        @pl.when(moving)
        def _():
            gather_pieces()

    if may_f or may_p:

        @pl.when(in_flight(b_f))
        def _():
            project(b_f)

    if may_f:

        @pl.when(in_flight(b_f) & jnp.logical_not(last))
        def _():
            def one_group(group):
                q_three, keys, values = group_operands(group, b_f)
                probs = probabilities(q_three, keys, count)
                heads = mixdot(probs.astype(BF16), values).astype(BF16)
                for k in range(PER):
                    mixed[:, lanes(group * PER + k)] = heads[k * count : (k + 1) * count]

            several(GROUPS, one_group, UNROLL_GROUPS)
            for copy in copies[12:]:
                copy.wait()

            def out_tile(n, carry):
                cols = pl.ds(pl.multiple_of(n * 512, 512), 512)
                part[:, cols] = mixdot(mixed[...], wo[0, :, cols]).astype(BF16)
                return carry

            lax.fori_loop(0, width // 512, out_tile, 0)

    if may_b:
        if may_p:

            @pl.when(do_b & last)
            def _():
                gbuf[...] = cot[b_b]

        @pl.when(do_b)
        def _():
            def grad_tile(j):
                rows = columns(j)
                mixed[:, rows] = dot_nt(gbuf[...], wo[0, rows]).astype(BF16)

            several(3, grad_tile, tick >= UNROLL_GRADS)

            def one_group(group):
                q_three, keys, values = group_operands(group, b_b)
                probs = probabilities(q_three, keys, count)
                heads = [mixed[:, lanes(group * PER + k)] for k in range(PER)]
                g_three = jnp.concatenate(heads, axis=0)
                grad_probs = dot_nt(g_three, values)
                grad_values = dot_tn(probs.astype(BF16), g_three).astype(BF16)
                centre = jnp.sum(probs * grad_probs, axis=-1, keepdims=True)
                scaled = (probs * (grad_probs - centre) * SCALE).astype(BF16)
                grad_query = mixdot(scaled, keys).astype(BF16)
                grad_keys = dot_tn(scaled, q_three).astype(BF16)
                for k in range(PER):
                    head = group * PER + k
                    gtile[:, lanes(head)] = grad_query[k * count : (k + 1) * count]
                cols = lanes(group)
                gtile[:, lanes(GROUPS * PER + group)] = grad_keys[:count]
                gtile[:, lanes(GROUPS * PER + GROUPS + group)] = grad_values[:count]
                kept_slot[b_b, 0, :, cols] = grad_keys[count : count + SLOTS]
                kept_slot[b_b, 1, :, cols] = grad_values[count : count + SLOTS]

            several(GROUPS, one_group, UNROLL_GROUPS)

        if tick == TICKS - 1:
            for d in range(ends.shape[0]):
                ends[d] = kept_slot[...]

        if tick < TICKS - 1:

            @pl.when(do_b & (section > 0))
            def _():
                def in_tile(n, carry):
                    cols = pl.ds(pl.multiple_of(n * 512, 512), 512)
                    part[:, cols] = dot_nt(gtile[...], w_all[cols]).astype(BF16)
                    return carry

                lax.fori_loop(0, width // 512, in_tile, 0)


def kept_before(tick):
    return 0 if tick == 0 else (2 if tick <= SECTIONS - 1 else 3)


def run_tick(tick, info, gain, operands, shapes, pieces, kept):
    count, width, heads = shapes["sizes"]
    share = count // MP
    keep = [
        jax.ShapeDtypeStruct((MICRO, 5, count, TILE), BF16),
        jax.ShapeDtypeStruct((MICRO, share, width), BF16),
    ]
    if tick >= SECTIONS - 1:
        keep.append(jax.ShapeDtypeStruct((MICRO, 2, SLOTS, TILE), BF16))
    ends = []
    if tick == TICKS - 1:
        ends.append(jax.ShapeDtypeStruct((shapes["parts"], *keep[2].shape), BF16))
    operands = operands + list(pieces)
    first_kept = 2 + len(operands)
    given = shapes["given"] if tick == 0 else []
    in_specs = [SMEM] + [VMEM] * (1 + len(operands) + len(kept))
    if tick == 0:
        in_specs[1:] = [HBM] * 11
    scratch = [
        pltpu.VMEM((count, width), BF16),
        pltpu.VMEM((count, width), BF16),
        pltpu.VMEM((count, heads), BF16),
        pltpu.VMEM((count, 5 * TILE), BF16),
    ]
    if tick == 0:
        scratch += [pltpu.VMEM(array.shape, BF16) for array in operands[5:]]
        scratch.append(pltpu.SemaphoreType.DMA((14,)))
    return pl.pallas_call(
        functools.partial(tick_kernel, tick, count),
        out_shape=given + [jax.ShapeDtypeStruct((count, width), BF16)] + keep + ends,
        in_specs=in_specs,
        out_specs=[VMEM] * (len(given) + 1 + len(keep) + len(ends)),
        scratch_shapes=scratch,
        input_output_aliases={first_kept + i: 1 + i for i in range(len(kept))},
        compiler_params=pltpu.CompilerParams(
            vmem_limit_bytes=VMEM_FIRST if tick == 0 else VMEM_TICK
        ),
        name=f"tick{tick}",
    )(info, gain, *operands, *kept)


def update_kernel(tick, share, *refs):
    may_f = tick <= SECTIONS - 2 + MICRO - 1
    may_b = tick >= SECTIONS - 1
    may_p = SECTIONS - 1 <= tick <= SECTIONS - 1 + MICRO - 1
    refs = list(refs)
    info, arrived, gain, own = refs[:4]
    del refs[:4]
    cot = refs.pop(0) if may_p else None
    piece = refs.pop(0) if tick >= SECTIONS else None
    _, out, slots = refs
    section = info[0]
    me = info[1]
    b_f = tick - section
    b_b = tick - (2 * SECTIONS - 2) + section
    last = section == SECTIONS - 1

    for spare, number in slot_rounds(tick):

        @pl.when(section == spare)
        def _():
            def take(k):
                source = slot_source(slot_members(info[2], number, k), number)
                slots[pl.ds(pl.multiple_of(source * share, share), share)] = arrived[k]

            several(MP, take, False)

    def summed(rows):
        total = arrived[0, rows].astype(F32)
        for k in range(1, MP):
            total = total + arrived[k, rows].astype(F32)
        return total

    def step_back(grad_of):
        def rows_of(i, carry):
            rows = pl.ds(pl.multiple_of(i * 16, 16), 16)
            wide = own[b_b, rows].astype(F32)
            inverse = lax.rsqrt(jnp.mean(wide * wide, axis=-1, keepdims=True) + EPS)
            unit = wide * inverse
            scaled = summed(rows) * gain[...]
            centre = jnp.mean(scaled * unit, axis=-1, keepdims=True)
            change = inverse * (scaled - unit * centre)
            out[rows] = (grad_of(i, rows).astype(F32) + change).astype(BF16)
            return carry

        lax.fori_loop(0, share // 16, rows_of, 0)

    if may_f:

        @pl.when(in_flight(b_f) & jnp.logical_not(last))
        def _():
            def rows_of(i, carry):
                rows = pl.ds(pl.multiple_of(i * 16, 16), 16)
                out[rows] = (own[b_f, rows].astype(F32) + summed(rows)).astype(BF16)
                return carry

            lax.fori_loop(0, share // 16, rows_of, 0)

    if may_b:

        @pl.when(in_flight(b_b) & (section > 0))
        def _():
            def grad_of(i, rows):
                if not may_p:
                    return piece[rows]
                given = cot[b_b, pl.ds(pl.multiple_of(me * share + i * 16, 16), 16)]
                if tick == SECTIONS - 1:
                    return given
                return jnp.where(last, given.astype(F32), piece[rows].astype(F32))

            step_back(grad_of)


def run_update(tick, info, arrived, gain, own, cot, piece, slots):
    share, width = arrived.shape[1:]
    operands = [arrived, gain, own]
    if SECTIONS - 1 <= tick <= SECTIONS - 1 + MICRO - 1:
        operands.append(cot)
    if tick >= SECTIONS:
        operands.append(piece)
    operands.append(slots)
    return pl.pallas_call(
        functools.partial(update_kernel, tick, share),
        out_shape=[
            jax.ShapeDtypeStruct((share, width), BF16),
            jax.ShapeDtypeStruct(slots.shape, BF16),
        ],
        in_specs=[SMEM] + [VMEM] * len(operands),
        out_specs=[VMEM] * 2,
        input_output_aliases={len(operands): 1},
        compiler_params=pltpu.CompilerParams(vmem_limit_bytes=VMEM_UPDATE),
        name=f"update{tick}",
    )(info, *operands)


def routes(tick, offset):
    pairs = []
    for section in range(SECTIONS):
        target = None
        if section < SECTIONS - 1 and 0 <= tick - section < MICRO:
            target = section + 1
        if section > 0 and 0 <= tick - (2 * SECTIONS - 2) + section < MICRO:
            target = section - 1
        if target is not None:
            for m in range(MP):
                pairs.append((section * MP + m, target * MP + (m + offset) % MP))
    return pairs


def sum_groups(tick, parts):
    found = []
    for section in range(SECTIONS):
        forward = section < SECTIONS - 1 and 0 <= tick - section < MICRO
        backward = section > 0 and 0 <= tick - (2 * SECTIONS - 2) + section < MICRO
        place = lambda d, m: (d * SECTIONS + section) * MP + m
        if forward or backward:
            found += [[place(d, m) for m in range(MP)] for d in range(parts)]
            continue
        if dict(slot_rounds(tick)).get(section, 0) == 0:
            sets = [[2 * k + low for k in range(MP)] for low in range(2)]
        else:
            sets = [[4 * high + k for k in range(MP)] for high in range(2)]
        found += [[place(d, m) for d in members] for members in sets for m in range(MP)]
    return found


def grads_of(grads, kind):
    blocks = [grads[d, block, kind] for d in range(grads.shape[0]) for block in range(MICRO)]
    return jnp.concatenate(blocks, axis=0)


def lows_kernel(grads, key_b, value_b, out):
    low_key = dot_nt(grads_of(grads, 0), key_b[...])
    low_value = dot_nt(grads_of(grads, 1), value_b[...])
    total = jnp.concatenate([low_key, low_value], axis=1).astype(BF16)
    for k in range(MP):
        out[k] = total


def run_lows(grads, key_b, value_b):
    rows = grads.shape[0] * MICRO * SLOTS
    return pl.pallas_call(
        lows_kernel,
        out_shape=jax.ShapeDtypeStruct((MP, rows, 2 * key_b.shape[0]), BF16),
        in_specs=[VMEM] * 3,
        out_specs=VMEM,
        compiler_params=pltpu.CompilerParams(vmem_limit_bytes=VMEM_END),
        name="lows",
    )(grads, key_b, value_b)


def grad_b_kernel(slots, grads, key_a, value_a, out):
    for kind, down in enumerate((key_a, value_a)):
        low = dot_nt(slots[...], down[...]).astype(BF16)
        out[kind] = dot_tn(low, grads_of(grads, kind))


def run_grad_b(slots, grads, key_a, value_a):
    rank, width = key_a.shape
    return pl.pallas_call(
        grad_b_kernel,
        out_shape=jax.ShapeDtypeStruct((2, rank, grads.shape[-1]), F32),
        in_specs=[VMEM] * 4,
        out_specs=VMEM,
        compiler_params=pltpu.CompilerParams(vmem_limit_bytes=VMEM_END),
        cost_estimate=pl.CostEstimate(
            flops=4 * slots.shape[0] * rank * width, bytes_accessed=1 << 22, transcendentals=0
        ),
        name="grad_b",
    )(slots, grads, key_a, value_a)


def grad_a_kernel(lows, slots, out):
    total = lows[0].astype(F32)
    for k in range(1, MP):
        total = total + lows[k].astype(F32)
    total = total.astype(BF16)

    out[...] = mixdot(total.T, slots[...])


def run_grad_a(lows, slots):
    return pl.pallas_call(
        grad_a_kernel,
        out_shape=jax.ShapeDtypeStruct((lows.shape[2], slots.shape[1]), F32),
        grid=(4,),
        in_specs=[
            pl.BlockSpec(lows.shape, lambda n: (0, 0, 0)),
            pl.BlockSpec((slots.shape[0], slots.shape[1] // 4), lambda n: (0, n)),
        ],
        out_specs=pl.BlockSpec((lows.shape[2], slots.shape[1] // 4), lambda n: (0, n)),
        compiler_params=pltpu.CompilerParams(vmem_limit_bytes=VMEM_END),
        name="grad_a",
    )(lows, slots)


def local(
    hidden_in,
    slot_hidden,
    norm_gain,
    w_query,
    w_key,
    w_value,
    w_out,
    key_a,
    key_b,
    value_a,
    value_b,
    cotangent,
):
    width = hidden_in.shape[2]
    share = hidden_in.shape[1] // MP
    places = [lax.axis_index(name) for name in ("section", "mp", "dp")]
    info = jnp.stack(places).astype(jnp.int32)
    parts = lax.axis_size("dp")

    like = lambda array: jax.ShapeDtypeStruct(array.shape, BF16)
    block_rows = jax.ShapeDtypeStruct(hidden_in.shape[1:], BF16)
    shapes = {
        "parts": parts,
        "sizes": (*hidden_in.shape[1:], w_query.shape[2]),
        "given": [
            jax.ShapeDtypeStruct(norm_gain.shape, F32),
            block_rows,
            jax.ShapeDtypeStruct((width, 5 * TILE), BF16),
            like(w_out),
            jax.ShapeDtypeStruct((MICRO, 2, SLOTS, TILE), BF16),
            jax.ShapeDtypeStruct((parts * MICRO * SLOTS, width), BF16),
        ],
    }
    pieces = []
    kept = []
    for tick in range(TICKS):
        if tick == 0:
            operands = [hidden_in, w_key, w_value, w_query, w_out]
            operands += [slot_hidden[0].reshape(-1, width), key_a[0].T, key_b[0]]
            operands += [value_a[0].T, value_b[0]]
            far = [pltpu.with_memory_space_constraint(x, pltpu.HBM) for x in [norm_gain] + operands]
            found = run_tick(tick, info, far[0], far[1:], shapes, [], [])
            gain, late, w_all, wo, slot_kv, slots = found[:6]
            part, *kept = found[6:]
        else:
            operands = [slot_kv, wo] + ([slots, w_all] if tick < TICKS - 1 else [])
            if tick < MICRO:
                operands.append(late)
            if SECTIONS - 1 <= tick <= SECTIONS - 1 + MICRO - 1:
                operands.append(cotangent)
            part, *kept = run_tick(tick, info, gain, operands, shapes, pieces, kept)
        if tick + 1 < TICKS:
            arrived = lax.all_to_all(
                part.reshape(MP, share, width),
                ("dp", "section", "mp"),
                0,
                0,
                axis_index_groups=sum_groups(tick, lax.axis_size("dp")),
                tiled=True,
            )
            own_piece = pieces[0] if pieces else None
            send, slots = run_update(
                tick, info, arrived, gain, kept[1], cotangent, own_piece, slots
            )
            sent = {
                offset: lax.ppermute(send, ("section", "mp"), routes(tick, offset))
                for offset in (2, 1, 3, 0)
            }
            pieces = [sent[offset] for offset in range(MP)]
    with jax.named_scope("ends"):
        all_grads = lax.all_to_all(kept[3], "dp", 0, 0, tiled=True)
    up = (key_b[0], value_b[0])
    lows = run_lows(all_grads, *up)
    with jax.named_scope("lows"):
        lows = lax.all_to_all(lows, "mp", 0, 0, tiled=True)
    grad_b = run_grad_b(slots, all_grads, key_a[0].T, value_a[0].T)
    grad_a = run_grad_a(lows, slots).reshape(2, -1, width)
    return (jnp.swapaxes(grad_a, 1, 2)[None], grad_b[None])


def solution(mesh):
    placed = (
        P("dp", None, None),
        P("section", "dp", None, None),
        P("section", None),
        P("section", None, "mp"),
        P("section", None, "mp"),
        P("section", None, "mp"),
        P("section", "mp", None),
        P("section", None, None),
        P("section", None, "mp"),
        P("section", None, None),
        P("section", None, "mp"),
        P("dp", None, None),
    )
    return jax.shard_map(
        local,
        mesh=mesh,
        in_specs=placed,
        out_specs=(P("section", None, None, None), P("section", None, None, "mp")),
        check_vma=False,
    )
```
